256 devices in a mesh: ctx: 32 (over x, y, core), head: 8 (over z).
Axes of the slice: x: 4, y: 4, z: 8, core: 2. Of those that a mesh axis runs over, the one named last changes fastest.
Arguments:
- queries: bfloat16 [65536, 2048], P(('ctx', 'head')), may hold values from -6 to 6
- key_vectors: bfloat16 [65536, 2048], P(('ctx', 'head')), may hold values from -6 to 6
- value_vectors: bfloat16 [65536, 2048], P(('ctx', 'head')), may hold values from -6 to 6
- level_codes: int32 [65536, 6], P('ctx'), may hold values from 0 to 15
- level_table: bfloat16 [16, 16], replicated, may hold values from 0.25 to 2
- out_gain: float32 [16, 128], replicated, may hold values from 0.5 to 1.5
Outputs:
- attended: bfloat16 [65536, 2048], P(('ctx', 'head'))
The draws below stay inside these ranges and needn't reach their ends.
All inputs are finite; a program needn't handle non-finite values.
Results may differ from the reference program's by a relative error of at most 0.005.
Values may be sent and summed in bfloat16 or wider, within the bound.
No kernel may reach another device: no remote copies, remote signals or barrier semaphores. Data moves between devices by JAX's collectives and lax.ppermute only.
A program may use at most 64 MiB of HBM per device.

```python
import jax
import jax.numpy as jnp
from jax import lax

HEADS = 16
DH = 128
CODES = 16
BLOCK = 2048
SPAN = 512
TOKENS = 65536
CTX_LEVELS = 5
LEVELS = 6
N_CTX = 32


def with_ends(entries, own_key, least, top_value):
    index_at = [jax.random.randint(jax.random.fold_in(own_key, axis), (), 0, length) for axis, length in enumerate(entries.shape)]
    main_axis = entries.shape.index(max(entries.shape))
    next_to = index_at[:main_axis] + [(index_at[main_axis] + 1) % entries.shape[main_axis]] + index_at[main_axis + 1:]
    return entries.at[tuple(index_at)].set(least).at[tuple(next_to)].set(top_value)


def shard_levels(stream_key, extent, split, low, top_value):
    loudness, own = 1.0, jax.random.fold_in(stream_key, 6)
    for position, parts in split:
        heights = jnp.exp(jax.random.uniform(jax.random.fold_in(own, position), (parts,), jnp.float32, low / len(split), top_value / len(split)))
        loudness = loudness * jnp.repeat(heights, extent[position] // parts).reshape([-1 if axis == position else 1 for axis in range(len(extent))])
    return loudness


def normal_values(key, dims, spread, reach, shards=(), held_as=jnp.bfloat16):
    array = spread * jax.random.normal(key, dims, jnp.float32)
    if shards:
        array = array * shard_levels(key, dims, shards, -0.22, 0.18)
    return jnp.clip(array, -reach, reach).astype(held_as)


def setup_inputs(seed: int = 0) -> dict:
    key_list = jax.random.split(jax.random.key(seed), 7)
    return {
        "queries": normal_values(key_list[0], (TOKENS, HEADS * DH), 1.0, 6.0, ((0, 256),)),
        "key_vectors": normal_values(key_list[1], (TOKENS, HEADS * DH), 1.0, 6.0, ((0, 256),)),
        "value_vectors": normal_values(key_list[2], (TOKENS, HEADS * DH), 1.0, 6.0, ((0, 256),)),
        "level_codes": with_ends(jax.random.randint(key_list[3], (TOKENS, LEVELS), 0, CODES), jax.random.fold_in(key_list[3], 1), 0, CODES - 1).astype(jnp.int32),
        "level_table": jnp.clip(jax.random.uniform(key_list[4], (CODES, HEADS), jnp.float32, 0.25, 2.0), 0.25, 2.0).astype(jnp.bfloat16),
        "out_gain": jnp.clip(1.0 + 0.1 * jax.random.normal(key_list[5], (HEADS, DH), jnp.float32), 0.5, 1.5),
    }


epsilon = 1e-06

def rounded(array_in):
    return lax.optimization_barrier(array_in.astype(jnp.bfloat16)).astype(jnp.float32)

def level_select(own_block, other_blocks, level_index):
    high_same = own_block >> level_index + 1 == other_blocks >> level_index + 1
    own_set = own_block >> level_index & 1 == 1
    other_clear = other_blocks >> level_index & 1 == 0
    return (high_same & own_set & other_clear).astype(jnp.float32)

def block_level0(query_block, key_block, value_block):
    span_count = query_block.shape[0] // SPAN
    query_spans = query_block.reshape(span_count, SPAN, HEADS, DH).astype(jnp.float32)
    key_spans = key_block.reshape(span_count, SPAN, HEADS, DH).astype(jnp.float32)
    value_spans = value_block.reshape(span_count, SPAN, HEADS, DH).astype(jnp.float32)
    scores = jnp.einsum('cqhd,ckhd->chqk', query_spans, key_spans)
    row_ids = lax.broadcasted_iota(jnp.int32, (SPAN, SPAN), 0)
    col_ids = lax.broadcasted_iota(jnp.int32, (SPAN, SPAN), 1)
    masked = rounded(jnp.where(col_ids <= row_ids, scores, jnp.zeros_like(scores)))
    local = jnp.einsum('chqk,ckhd->cqhd', masked, value_spans)
    span_states = jnp.einsum('ckhd,ckhe->chde', key_spans, value_spans)
    running = jnp.cumsum(span_states, axis=0)
    prefix = jnp.concatenate([jnp.zeros_like(span_states[:1]), running[:-1]], axis=0)
    carried = jnp.einsum('cqhd,chde->cqhe', query_spans, rounded(prefix))
    return (local + carried).reshape(query_block.shape[0], HEADS, DH)

def reference(queries, key_vectors, value_vectors, level_codes, level_table, out_gain):
    query_blocks = queries.reshape(N_CTX, BLOCK, HEADS, DH)
    key_blocks = key_vectors.reshape(N_CTX, BLOCK, HEADS, DH)
    value_blocks = value_vectors.reshape(N_CTX, BLOCK, HEADS, DH)
    code_blocks = level_codes.reshape(N_CTX, BLOCK, LEVELS)

    def state_of(pair):
        return jnp.einsum('thd,the->hde', pair[0].astype(jnp.float32), pair[1].astype(jnp.float32))
    block_states = lax.map(state_of, (key_blocks, value_blocks))
    block_ids = jnp.arange(N_CTX, dtype=jnp.int32)
    table = level_table.astype(jnp.float32)

    def one_block(inputs):
        block_index, query_block, key_block, value_block, code_block = inputs
        level0 = block_level0(query_block, key_block, value_block)
        weights = table[code_block]
        combined = weights[:, 0, :, None] * level0
        query_float = query_block.astype(jnp.float32)
        for level_index in range(CTX_LEVELS):
            selector = level_select(block_index, block_ids, level_index)
            state = jnp.einsum('n,nhde->hde', selector, block_states, precision=lax.Precision.HIGHEST)
            level_reads = jnp.einsum('thd,hde->the', query_float, rounded(state))
            combined = combined + weights[:, level_index + 1, :, None] * level_reads
        inverse_rms = lax.rsqrt(lax.optimization_barrier(jnp.mean(combined * combined, axis=-1, keepdims=True)) + epsilon)
        normed = combined * inverse_rms * out_gain.astype(jnp.float32)
        return normed.astype(jnp.bfloat16).reshape(BLOCK, HEADS * DH)
    attended = lax.map(one_block, (block_ids, query_blocks, key_blocks, value_blocks, code_blocks))
    return attended.reshape(TOKENS, HEADS * DH)
```

```python
import jax
import jax.numpy as jnp
from jax import lax
from jax.experimental import pallas as pl
from jax.experimental.pallas import tpu as pltpu
from jax.sharding import Mesh, PartitionSpec as P

HEADS = 16
DH = 128
LEVELS = 6
CODES = 16
EPSILON = 1e-06
BF = jnp.bfloat16
F32 = jnp.float32


VMEM_SPEC = pl.BlockSpec(memory_space=pltpu.VMEM)
SMEM_SPEC = pl.BlockSpec(memory_space=pltpu.SMEM)


def call(kernel, outs, n_in, flops, nbytes, name, smem=0, vmem=32 << 20):
    return pl.pallas_call(
        kernel,
        out_shape=outs,
        in_specs=[SMEM_SPEC] * smem + [VMEM_SPEC] * n_in,
        out_specs=jax.tree.map(lambda _: VMEM_SPEC, outs),
        compiler_params=pltpu.CompilerParams(vmem_limit_bytes=vmem),
        cost_estimate=pl.CostEstimate(flops=flops, bytes_accessed=nbytes, transcendentals=0),
        name=name,
    )


def sds(shape, dtype):
    return jax.ShapeDtypeStruct(shape, dtype)


def head_cols(h):
    return pl.ds(h * DH, DH)


def state_kernel(k_ref, v_ref, s_ref):
    for h in range(HEADS):
        s = lax.dot_general(
            k_ref[:, head_cols(h)], v_ref[:, head_cols(h)], (((0,), (0,)), ((), ())),
            preferred_element_type=F32,
        )
        s_ref[h] = s.astype(BF)


def local_kernel(core_ref, q_ref, k_ref, v_ref, codes_ref, table_ref, local_ref, w_ref):
    tokens = q_ref.shape[0]
    head_of = lax.broadcasted_iota(jnp.int32, (HEADS, HEADS * DH), 1) // DH
    row_of = lax.broadcasted_iota(jnp.int32, (HEADS, HEADS * DH), 0)
    spread = jnp.where(head_of == row_of, 1.0, 0.0).astype(BF)
    table = jnp.dot(table_ref[...], spread, preferred_element_type=F32).astype(BF)
    code_ids = lax.broadcasted_iota(jnp.int32, (CODES, tokens), 0)
    for l in range(LEVELS):
        hit = codes_ref[l : l + 1, :] == code_ids
        if l == 1:
            hit = hit & (core_ref[0] == 1)
        onehot = jnp.where(hit, 1.0, 0.0).astype(BF)
        w = lax.dot_general(onehot, table, (((0,), (0,)), ((), ())), preferred_element_type=F32)
        w_ref[l] = w.astype(BF)
    rows = lax.broadcasted_iota(jnp.int32, (tokens, tokens), 0)
    cols = lax.broadcasted_iota(jnp.int32, (tokens, tokens), 1)
    keep = cols <= rows
    for h in range(HEADS):
        s = lax.dot_general(
            q_ref[:, head_cols(h)], k_ref[:, head_cols(h)], (((1,), (1,)), ((), ())),
            preferred_element_type=F32,
        )
        s = jnp.where(keep, s, 0.0).astype(BF)
        local_ref[:, head_cols(h)] = jnp.dot(s, v_ref[:, head_cols(h)], preferred_element_type=F32)


def prefix_kernel(core_ref, r_ref, p_ref, t_ref, mine_ref, send_ref):
    run = jnp.zeros(r_ref.shape[1:], F32)
    for j in range(r_ref.shape[0]):
        p_ref[j] = run.astype(BF)
        run = run + r_ref[j].astype(F32)
    t_ref[...] = run
    core = core_ref[0]
    mine_ref[...] = t_ref[core]
    send_ref[...] = t_ref[1 - core].astype(send_ref.dtype)


def carry_kernel(q_ref, p_ref, local_ref, w_ref, acc_ref):
    for h in range(HEADS):
        read = jnp.dot(q_ref[:, head_cols(h)], p_ref[h], preferred_element_type=F32)
        w = w_ref[0, :, head_cols(h)].astype(F32)
        acc_ref[:, head_cols(h)] = w * (local_ref[:, head_cols(h)] + read)


def final_kernel(zc_ref, q_ref, acc_ref, w_ref, gain_ref, *refs):
    levels, out_ref = refs[:-1], refs[-1]
    z, core = zc_ref[0], zc_ref[1]
    for d in range(8):
        for other in range(2):
            a, b = levels[2 * (2 * d + other)], levels[2 * (2 * d + other) + 1]
            owner = lax.rem(z + 8 - d, 8)
            hh = core if other == 0 else 1 - core
            h = owner * 2 + hh
            cols = pl.ds(pl.multiple_of(h * DH, DH), DH)
            q = q_ref[:, cols]
            total = acc_ref[:, cols]
            states = [a[0], a[1], a[2], b[0], b[1]]
            for l in range(5):
                read = jnp.dot(q, states[l], preferred_element_type=F32)
                total = total + w_ref[l + 1, :, cols].astype(F32) * read
            inv = lax.rsqrt(jnp.mean(total * total, axis=-1, keepdims=True) + EPSILON)
            out_ref[:, cols] = (total * inv * gain_ref[pl.ds(h, 1), :]).astype(BF)


def shift(n, s):
    return [(i, (i + s) % n) for i in range(n)]


def select_levels(axis, total, wire):
    sent = total.astype(wire)
    idx = lax.axis_index(axis)
    a1 = lax.ppermute(sent, axis, shift(4, 1))
    a3 = lax.ppermute(sent, axis, shift(4, 3))
    a2 = lax.ppermute(sent, axis, shift(4, 2))
    zero = jnp.zeros_like(total)
    a1, a2, a3 = a1.astype(F32), a2.astype(F32), a3.astype(F32)
    low = jnp.where(idx % 2 == 1, a1, zero)
    high = jnp.where(idx >= 2, a2 + jnp.where(idx == 2, a1, a3), zero)
    return low.astype(BF), high.astype(BF), total + a1 + a2 + a3


def body(queries, key_vectors, value_vectors, level_codes, level_table, out_gain):
    tokens = queries.shape[0]
    z = lax.axis_index("z")
    core = lax.axis_index("core")
    codes = lax.dynamic_slice_in_dim(level_codes.T, z * tokens, tokens, 1)

    states = call(state_kernel, sds((HEADS, DH, DH), BF), 2, 2 * tokens * HEADS * DH * DH, 3 << 20, "chunk_states")(
        key_vectors, value_vectors
    )
    gathered = lax.all_to_all(states, "z", split_axis=0, concat_axis=0, tiled=True)

    local, weights = call(
        local_kernel,
        (sds((tokens, HEADS * DH), F32), sds((LEVELS, tokens, HEADS * DH), BF)),
        5, 4 * tokens * tokens * HEADS * DH, 11 << 20, "local_part", smem=1,
    )(core[None], queries, key_vectors, value_vectors, codes, level_table)
    gathered, local, weights = lax.optimization_barrier((gathered, local, weights))

    wire = BF
    prefixes, _, mine, send = call(
        prefix_kernel,
        (sds((8, 2, DH, DH), BF), sds((2, DH, DH), F32), sds((DH, DH), F32), sds((DH, DH), wire)),
        1, 8 * 2 * DH * DH, 1 << 20, "prefix_sums", smem=1,
    )(core[None], gathered.reshape(8, 2, DH, DH))
    prefix = lax.all_to_all(prefixes.reshape(HEADS, DH, DH), "z", split_axis=0, concat_axis=0, tiled=True)

    other = lax.ppermute(send, "core", shift(2, 1)).astype(F32)
    level0 = jnp.where(core == 0, mine, other).astype(BF)
    level1, level2, total = select_levels("y", mine + other, wire)
    group_a = jnp.stack([level0, level1, level2])
    level3, level4, _ = select_levels("x", total, wire)
    group_b = jnp.stack([level3, level4])

    got = {}
    for name, own, extra in (("a", group_a, 1), ("b", group_b, -1)):
        got[name, 0] = own
        for step in (1, -1):
            moving = own
            for hop in range(1, 5 if step == extra else 4):
                moving = lax.ppermute(moving, "z", shift(8, step))
                got[name, (hop * step) % 8] = moving
    operands = []
    for d in range(8):
        pair = [got["a", d], got["b", d]]
        operands += pair
        operands += [lax.ppermute(p, "core", shift(2, 1)) for p in pair]

    acc = call(
        carry_kernel, sds((tokens, HEADS * DH), F32), 4, 2 * tokens * HEADS * DH * DH, 6 << 20, "prefix_part",
    )(queries, prefix, local, weights)
    return call(
        final_kernel, sds((tokens, HEADS * DH), BF), 4 + len(operands), 10 * tokens * HEADS * DH * DH, 11 << 20,
        "level_part", smem=1,
    )(jnp.stack([z, core]).astype(jnp.int32), queries, acc, weights, out_gain, *operands)


def solution(mesh):
    grid = Mesh(mesh.devices.reshape(4, 4, 2, 8), ("x", "y", "core", "z"))
    rows = P(("x", "y", "core", "z"), None)
    in_specs = (rows, rows, rows, P(("x", "y", "core"), None), P(), P())
    return jax.shard_map(body, mesh=grid, in_specs=in_specs, out_specs=rows, check_vma=False)
```

```python
import functools

import jax
import jax.numpy as jnp
from jax import lax
from jax.experimental import pallas as pl
from jax.experimental.pallas import tpu as pltpu
from jax.sharding import Mesh, PartitionSpec as P

HEADS = 16
DH = 128
LEVELS = 6
CODES = 16
NEAR = 3
SIDE = 8
PER = HEADS // SIDE
EPSILON = 1e-06
BF = jnp.bfloat16
F32 = jnp.float32


VMEM_SPEC = pl.BlockSpec(memory_space=pltpu.VMEM)
SMEM_SPEC = pl.BlockSpec(memory_space=pltpu.SMEM)
HBM_SPEC = pl.BlockSpec(memory_space=pltpu.HBM)
DMA = pltpu.SemaphoreType.DMA


def sds(shape, dtype):
    return jax.ShapeDtypeStruct(shape, dtype)


def call(kernel, outs, in_specs, name, cost, out_specs=None, scratch=(), alias=None):
    return pl.pallas_call(
        kernel,
        out_shape=outs,
        in_specs=in_specs,
        out_specs=jax.tree.map(lambda _: VMEM_SPEC, outs) if out_specs is None else out_specs,
        scratch_shapes=scratch,
        input_output_aliases=alias or {},
        compiler_params=pltpu.CompilerParams(vmem_limit_bytes=16 << 20),
        cost_estimate=pl.CostEstimate(flops=cost[0], bytes_accessed=cost[1], transcendentals=0),
        name=name,
    )


def in_hbm(value):
    return pltpu.with_memory_space_constraint(value, pltpu.HBM)


def head_cols(h):
    return pl.ds(h * DH, DH)


def dynamic_cols(h):
    return pl.ds(pl.multiple_of(h * DH, DH), DH)


LOADS = 4


def state_kernel(k_hbm, v_hbm, s_ref, k_ref, v_ref, sems):
    width = HEADS * DH // LOADS
    copies = []
    for i in range(LOADS):
        cols = pl.ds(i * width, width)
        pair = [
            pltpu.make_async_copy(k_hbm.at[:, cols], k_ref.at[:, cols], sems.at[0, i]),
            pltpu.make_async_copy(v_hbm.at[:, cols], v_ref.at[:, cols], sems.at[1, i]),
        ]
        for copy in pair:
            copy.start()
        copies.append(pair)
    for i in range(LOADS):
        for copy in copies[i]:
            copy.wait()
        for h in range(i * HEADS // LOADS, (i + 1) * HEADS // LOADS):
            s = lax.dot_general(
                k_ref[:, head_cols(h)], v_ref[:, head_cols(h)], (((0,), (0,)), ((), ())),
                preferred_element_type=F32,
            )
            s_ref[h] = s.astype(BF)


def local_kernel(q_hbm, k_hbm, v_hbm, codes_ref, table_ref, acc_hbm, w_hbm, q_ref, k_ref, v_ref, acc_ref, w_ref, sems, out_sems):
    width = HEADS * DH // LOADS
    per = HEADS // LOADS
    copies = []
    for i in range(LOADS):
        cols = pl.ds(i * width, width)
        group = [
            pltpu.make_async_copy(src.at[:, cols], dst.at[:, cols], sems.at[j, i])
            for j, (src, dst) in enumerate(((q_hbm, q_ref), (k_hbm, k_ref), (v_hbm, v_ref)))
        ]
        for copy in group:
            copy.start()
        copies.append(group)
    tokens = q_ref.shape[0]
    code_ids = lax.broadcasted_iota(jnp.int32, (CODES, tokens), 0)
    hits = [codes_ref[l : l + 1, :] == code_ids for l in range(LEVELS)]
    hits = [jnp.where(hit, 1.0, 0.0).astype(BF) for hit in hits]
    hits = jnp.concatenate(hits + [jnp.zeros((DH - LEVELS * CODES, tokens), BF)], axis=0)
    w = lax.dot_general(hits, table_ref[...], (((0,), (0,)), ((), ())), preferred_element_type=F32)
    w_ref[...] = w
    stores = [pltpu.make_async_copy(w_ref, w_hbm, out_sems.at[LOADS])]
    stores[0].start()
    rows = lax.broadcasted_iota(jnp.int32, (tokens, tokens), 0)
    cols = lax.broadcasted_iota(jnp.int32, (tokens, tokens), 1)
    keep = cols <= rows
    for i in range(LOADS):
        for copy in copies[i]:
            copy.wait()
        for h in range(i * per, (i + 1) * per):
            s = lax.dot_general(
                q_ref[:, head_cols(h)], k_ref[:, head_cols(h)], (((1,), (1,)), ((), ())),
                preferred_element_type=F32,
            )
            s = jnp.where(keep, s, 0.0).astype(BF)
            part = jnp.dot(s, v_ref[:, head_cols(h)], preferred_element_type=F32)
            acc_ref[:, head_cols(h)] = w[:, h : h + 1] * part
        cols = pl.ds(i * width, width)
        store = pltpu.make_async_copy(acc_ref.at[:, cols], acc_hbm.at[:, cols], out_sems.at[i])
        store.start()
        stores.append(store)
    for store in stores:
        store.wait()


def total_kernel(r_ref, mine_ref):
    run = r_ref[0].astype(F32)
    for j in range(1, SIDE):
        run = run + r_ref[j].astype(F32)
    mine_ref[...] = run


def prefix_kernel(r_ref, p_ref):
    run = jnp.zeros((PER * DH, DH), F32)
    for j in range(SIDE):
        p_ref[j] = run.astype(BF)
        run = run + r_ref[j].astype(F32)


def pair_kernel(mine_ref, other_ref, total_ref, sent_ref):
    total = mine_ref[...] + other_ref[...]
    total_ref[...] = total
    sent_ref[...] = total.astype(BF)


def on(flag, value):
    return (value * jnp.where(flag, 1.0, 0.0)).astype(BF)


def near_kernel(pos_ref, mine_ref, other_ref, total_ref, a1_ref, a2_ref, a3_ref, out_ref, sum_ref, sent_ref):
    y, core = pos_ref[1], pos_ref[2]
    a1, a2, a3 = a1_ref[...].astype(F32), a2_ref[...].astype(F32), a3_ref[...].astype(F32)
    two = jnp.where(y == 2, 1.0, 0.0)
    first = jnp.where(core == 0, 1.0, 0.0)
    out_ref[:, head_cols(0)] = (mine_ref[...] * first + other_ref[...] * (1.0 - first)).astype(BF)
    out_ref[:, head_cols(1)] = on(y % 2 == 1, a1)
    out_ref[:, head_cols(2)] = on(y >= 2, a2 + a1 * two + a3 * (1.0 - two))
    total = total_ref[...] + (a1 + a2 + a3)
    sum_ref[...] = total
    sent_ref[...] = total.astype(BF)


def far_kernel(pos_ref, a1_ref, a2_ref, a3_ref, out_ref):
    x = pos_ref[0]
    a1, a2, a3 = a1_ref[...].astype(F32), a2_ref[...].astype(F32), a3_ref[...].astype(F32)
    two = jnp.where(x == 2, 1.0, 0.0)
    out_ref[:, head_cols(0)] = on(x % 2 == 1, a1)
    out_ref[:, head_cols(1)] = on(x >= 2, a2 + a1 * two + a3 * (1.0 - two))


def step_kernel(order, first, pos_ref, *refs):
    refs = refs[0 if first else 1 :]
    q_hbm, acc_hbm, w_ref, p_hbm, gain_ref = refs[:5]
    count = len(order) * PER
    states = refs[5 : 5 + 2 * len(order)]
    out_hbm, q_ref, acc_ref, p_ref, o_ref, sems, out_sems = refs[5 + 2 * len(order) :]
    z, core = pos_ref[3], pos_ref[2]
    heads, loads = [], []
    for i in range(count):
        owner = lax.rem(z + order[i // PER] * (2 * core - 1) + SIDE, SIDE)
        h = owner * PER + i % PER
        copies = [
            pltpu.make_async_copy(q_hbm.at[:, dynamic_cols(h)], q_ref.at[i], sems.at[i, 0]),
            pltpu.make_async_copy(p_hbm.at[h], p_ref.at[i], sems.at[i, 1]),
            pltpu.make_async_copy(acc_hbm.at[:, dynamic_cols(h)], acc_ref.at[i], sems.at[i, 2]),
        ]
        for copy in copies:
            copy.start()
        heads.append(h)
        loads.append(copies)
    stores = []
    for i, h in enumerate(heads):
        w = pltpu.roll(w_ref[...], lax.rem(DH - h, DH), 1)
        for copy in loads[i]:
            copy.wait()
        q = q_ref[i]
        total = acc_ref[i] + w[:, :1] * jnp.dot(q, p_ref[i], preferred_element_type=F32)
        at = HEADS
        rows = slice(i % PER * DH, (i % PER + 1) * DH)
        for part in states[2 * (i // PER) : 2 * (i // PER) + 2]:
            reads = jnp.dot(q, part[rows, :], preferred_element_type=F32)
            for j in range(part.shape[1] // DH):
                total = total + w[:, at : at + 1] * reads[:, j * DH : (j + 1) * DH]
                at += HEADS
        inv = lax.rsqrt(jnp.mean(total * total, axis=-1, keepdims=True) + EPSILON)
        o_ref[i] = (total * inv * gain_ref[pl.ds(h, 1), :]).astype(BF)
        copy = pltpu.make_async_copy(o_ref.at[i], out_hbm.at[:, dynamic_cols(h)], out_sems.at[i])
        copy.start()
        stores.append(copy)
    for copy in stores:
        copy.wait()


def shift(n, s):
    return [(i, (i + s) % n) for i in range(n)]


SWAP = shift(2, 1)
RING = [(z, (z + 1) % 8) for z in range(8)] + [(8 + z, 8 + (z + 7) % 8) for z in range(8)]


def to_others(value, axis):
    a2 = lax.ppermute(value, axis, shift(4, 2))
    a1 = lax.ppermute(value, axis, shift(4, 1))
    a3 = lax.ppermute(value, axis, shift(4, 3))
    return a1, a2, a3


def swap(value):
    return lax.ppermute(value, "core", SWAP)


def body(queries, key_vectors, value_vectors, level_codes, level_table, out_gain):
    tokens = queries.shape[0]
    whole = (tokens, HEADS * DH)
    z = lax.axis_index("z")
    core = lax.axis_index("core").astype(jnp.int32)
    pos = jnp.stack([lax.axis_index("x"), lax.axis_index("y"), core, z]).astype(jnp.int32)
    codes = lax.dynamic_slice_in_dim(level_codes.T, z * tokens, tokens, 1)
    state = (PER * DH, DH)

    queries, key_vectors, value_vectors = (in_hbm(a) for a in (queries, key_vectors, value_vectors))
    states = call(
        state_kernel, sds((HEADS, DH, DH), BF), [HBM_SPEC] * 2, "chunk_states", (2 * tokens * HEADS * DH * DH, 3 << 20),
        scratch=[pltpu.VMEM(whole, BF), pltpu.VMEM(whole, BF), DMA((2, LOADS))],
    )(key_vectors, value_vectors)
    with jax.named_scope("gather_states"):
        gathered = lax.all_to_all(states, "z", split_axis=0, concat_axis=0, tiled=True)

    eye = jnp.eye(LEVELS, dtype=BF) * jnp.where(jnp.arange(LEVELS) == 1, core, 1).astype(BF)[:, None]
    table = jnp.kron(eye, level_table)
    table = jnp.pad(table, ((0, DH - LEVELS * CODES), (0, DH - LEVELS * HEADS)))
    acc, weights = call(
        local_kernel, (sds(whole, F32), sds((tokens, DH), F32)),
        [HBM_SPEC] * 3 + [VMEM_SPEC] * 2, "local_part", (4 * tokens * tokens * HEADS * DH, 6 << 20),
        out_specs=(HBM_SPEC, HBM_SPEC),
        scratch=[pltpu.VMEM(whole, BF)] * 3 + [
            pltpu.VMEM(whole, F32), pltpu.VMEM((tokens, DH), F32), DMA((3, LOADS)), DMA((LOADS + 1,)),
        ],
    )(queries, key_vectors, value_vectors, codes, table)
    gathered, acc, weights = lax.optimization_barrier((gathered, acc, weights))
    acc = in_hbm(acc)

    chunks = gathered.reshape((SIDE,) + state)
    mine = call(total_kernel, sds(state, F32), [VMEM_SPEC], "block_total", (8 * 2 * DH * DH, 1 << 20))(chunks)
    with jax.named_scope("core_swap"):
        other = swap(mine)
    prefixes = call(
        prefix_kernel, sds((SIDE,) + state, BF), [VMEM_SPEC], "prefix_sums", (8 * 2 * DH * DH, 1 << 20),
    )(chunks)
    with jax.named_scope("return_prefix"):
        prefix = lax.all_to_all(prefixes.reshape(HEADS, DH, DH), "z", split_axis=0, concat_axis=0, tiled=True)
    total, sent = call(
        pair_kernel, (sds(state, F32), sds(state, BF)), [VMEM_SPEC] * 2, "pair_total", (DH * DH, 1 << 18)
    )(mine, other)
    with jax.named_scope("y_phase"):
        around = to_others(sent, "y")
    near, _, sent = call(
        near_kernel, (sds((PER * DH, NEAR * DH), BF), sds(state, F32), sds(state, BF)), [SMEM_SPEC] + [VMEM_SPEC] * 6,
        "near_levels", (8 * DH * DH, 1 << 18),
    )(pos, mine, other, total, *around)
    with jax.named_scope("x_phase"):
        around = to_others(sent, "x")
    far = call(
        far_kernel, sds((PER * DH, 2 * DH), BF), [SMEM_SPEC] + [VMEM_SPEC] * 3, "far_levels", (8 * DH * DH, 1 << 18)
    )(pos, *around)

    def reads(hop, order, arrays, out):
        n = len(order) * PER
        return call(
            functools.partial(step_kernel, order, out is None), sds(whole, BF),
            [SMEM_SPEC] + ([] if out is None else [HBM_SPEC])
            + [HBM_SPEC, HBM_SPEC, VMEM_SPEC, HBM_SPEC] + [VMEM_SPEC] * (1 + len(arrays)),
            "reads_%d" % hop, (12 * tokens * n * DH * DH, n << 19),
            out_specs=HBM_SPEC,
            scratch=[
                pltpu.VMEM((n, tokens, DH), BF), pltpu.VMEM((n, tokens, DH), F32),
                pltpu.VMEM((n, DH, DH), BF), pltpu.VMEM((n, tokens, DH), BF), DMA((n, 3)), DMA((n,)),
            ],
            alias=None if out is None else {1: 0},
        )(pos, *([] if out is None else [out]), queries, acc, weights, prefix, out_gain, *arrays)

    a, b = near, far
    held = [((0,), [a, b])]
    for hop in range(1, 5):
        with jax.named_scope("ring"):
            a = lax.ppermute(a, ("core", "z"), RING)
            b = lax.ppermute(b, ("core", "z"), RING)
        with jax.named_scope("swap"):
            held.append(((hop, -hop), [a, b, swap(a), swap(b)]) if hop < 4 else ((hop,), [a, b]))
    out = None
    for hops in ((0, 1, 2), (3, 4)):
        order = sum((held[hop][0] for hop in hops), ())
        arrays = sum((held[hop][1] for hop in hops), [])
        out = reads(hops[0], order, arrays, out)
    return out


def solution(mesh):
    grid = Mesh(mesh.devices.reshape(4, 4, 2, 8), ("x", "y", "core", "z"))
    rows = P(("x", "y", "core", "z"), None)
    in_specs = (rows, rows, rows, P(("x", "y", "core"), None), P(), P())
    return jax.shard_map(body, mesh=grid, in_specs=in_specs, out_specs=rows, check_vma=False)
```

```python
import functools

import jax
import jax.numpy as jnp
from jax import lax
from jax.experimental import pallas as pl
from jax.experimental.pallas import tpu as pltpu
from jax.sharding import Mesh, PartitionSpec as P


HEADS = 16
DH = 128
LEVELS = 6
CODES = 16
NEAR = 3
FAR = 2
SIDE = 8
PER = HEADS // SIDE
EPSILON = 1e-06
BF = jnp.bfloat16
F32 = jnp.float32


VMEM_SPEC = pl.BlockSpec(memory_space=pltpu.VMEM)
SMEM_SPEC = pl.BlockSpec(memory_space=pltpu.SMEM)
HBM_SPEC = pl.BlockSpec(memory_space=pltpu.HBM)
DMA = pltpu.SemaphoreType.DMA


def sds(shape, dtype):
    return jax.ShapeDtypeStruct(shape, dtype)


def call(kernel, outs, in_specs, cost, out_specs=None, scratch=(), alias=None):
    return pl.pallas_call(
        kernel,
        out_shape=outs,
        in_specs=in_specs,
        out_specs=jax.tree.map(lambda _: VMEM_SPEC, outs) if out_specs is None else out_specs,
        scratch_shapes=scratch,
        input_output_aliases=alias or {},
        compiler_params=pltpu.CompilerParams(vmem_limit_bytes=20 << 20),
        cost_estimate=pl.CostEstimate(flops=cost[0], bytes_accessed=cost[1], transcendentals=0),
    )


def in_hbm(value):
    return pltpu.with_memory_space_constraint(value, pltpu.HBM)


def head_cols(h):
    return pl.ds(h * DH, DH)


def dynamic_cols(h):
    return pl.ds(pl.multiple_of(h * DH, DH), DH)


LOADS = 4


def state_kernel(k_hbm, v_hbm, s_ref, k_ref, v_ref, sems):
    width = HEADS * DH // LOADS
    copies = []
    for i in range(LOADS):
        cols = pl.ds(i * width, width)
        pair = [
            pltpu.make_async_copy(k_hbm.at[:, cols], k_ref.at[:, cols], sems.at[0, i]),
            pltpu.make_async_copy(v_hbm.at[:, cols], v_ref.at[:, cols], sems.at[1, i]),
        ]
        for copy in pair:
            copy.start()
        copies.append(pair)
    for i in range(LOADS):
        for copy in copies[i]:
            copy.wait()
        for h in range(i * HEADS // LOADS, (i + 1) * HEADS // LOADS):
            s = lax.dot_general(
                k_ref[:, head_cols(h)], v_ref[:, head_cols(h)], (((0,), (0,)), ((), ())),
                preferred_element_type=F32,
            )
            s_ref[h] = s.astype(BF)


def local_kernel(
    q_hbm, k_hbm, v_hbm, codes_ref, table_ref, acc_hbm, qw_hbm, q_ref, k_ref, v_ref, acc_ref, qw_ref, sems, acc_sems, qw_sems
):
    width = HEADS * DH // LOADS
    per = HEADS // LOADS
    copies = []
    for i in range(LOADS):
        cols = pl.ds(i * width, width)
        group = [
            pltpu.make_async_copy(src.at[:, cols], dst.at[:, cols], sems.at[j, i])
            for j, (src, dst) in enumerate(((q_hbm, q_ref), (k_hbm, k_ref), (v_hbm, v_ref)))
        ]
        for copy in group:
            copy.start()
        copies.append(group)
    tokens = q_ref.shape[0]
    code_ids = lax.broadcasted_iota(jnp.int32, (CODES, tokens), 0)
    hits = [codes_ref[l : l + 1, :] == code_ids for l in range(LEVELS)]
    hits = [jnp.where(hit, 1.0, 0.0).astype(BF) for hit in hits]
    hits = jnp.concatenate(hits + [jnp.zeros((DH - LEVELS * CODES, tokens), BF)], axis=0)
    w = lax.dot_general(hits, table_ref[...], (((0,), (0,)), ((), ())), preferred_element_type=F32).astype(BF)
    rows = lax.broadcasted_iota(jnp.int32, (tokens, tokens), 0)
    cols = lax.broadcasted_iota(jnp.int32, (tokens, tokens), 1)
    keep = cols <= rows
    pick = lax.broadcasted_iota(jnp.int32, (DH, LEVELS * DH), 0)
    pick = pick - lax.broadcasted_iota(jnp.int32, (DH, LEVELS * DH), 1) // DH * HEADS
    stores = []
    for i in range(LOADS):
        for copy in copies[i]:
            copy.wait()
        for h in range(i * per, (i + 1) * per):
            spread = jnp.dot(w, jnp.where(pick == h, 1.0, 0.0).astype(BF), preferred_element_type=F32)
            q = q_ref[:, head_cols(h)]
            wide = q.astype(F32)
            for l in range(LEVELS):
                qw_ref[h, :, head_cols(l)] = (spread[:, l * DH : (l + 1) * DH] * wide).astype(BF)
            s = lax.dot_general(q, k_ref[:, head_cols(h)], (((1,), (1,)), ((), ())), preferred_element_type=F32)
            s = jnp.where(keep, s, 0.0).astype(BF)
            part = jnp.dot(s, v_ref[:, head_cols(h)], preferred_element_type=F32)
            acc_ref[:, head_cols(h)] = spread[:, :DH] * part
        cols = pl.ds(i * width, width)
        heads = pl.ds(i * per, per)
        for store in (
            pltpu.make_async_copy(acc_ref.at[:, cols], acc_hbm.at[:, cols], acc_sems.at[i]),
            pltpu.make_async_copy(qw_ref.at[heads], qw_hbm.at[heads], qw_sems.at[i]),
        ):
            store.start()
            stores.append(store)
    for store in stores:
        store.wait()


def total_kernel(r_ref, mine_ref):
    run = r_ref[0].astype(F32)
    for j in range(1, SIDE):
        run = run + r_ref[j].astype(F32)
    mine_ref[...] = run


def prefix_kernel(r_ref, p_ref):
    run = jnp.zeros((PER * DH, DH), F32)
    for j in range(SIDE):
        p_ref[j] = run.astype(BF)
        run = run + r_ref[j].astype(F32)


def pair_kernel(mine_ref, other_ref, total_ref, sent_ref):
    total = mine_ref[...] + other_ref[...]
    total_ref[...] = total
    sent_ref[...] = total.astype(BF)


def on(flag, value):
    return (value * jnp.where(flag, 1.0, 0.0)).astype(BF)


def put(out_ref, l, count, value):
    for i in range(PER):
        at = (i * count + l) * DH
        out_ref[at : at + DH, :] = value[i * DH : (i + 1) * DH, :]


def near_kernel(pos_ref, mine_ref, other_ref, total_ref, a1_ref, a2_ref, a3_ref, out_ref, sum_ref, sent_ref):
    y, core = pos_ref[1], pos_ref[2]
    a1, a2, a3 = a1_ref[...].astype(F32), a2_ref[...].astype(F32), a3_ref[...].astype(F32)
    total = total_ref[...] + (a1 + a2 + a3)
    sum_ref[...] = total
    sent_ref[...] = total.astype(BF)
    two = jnp.where(y == 2, 1.0, 0.0)
    first = jnp.where(core == 0, 1.0, 0.0)
    put(out_ref, 0, NEAR, (mine_ref[...] * first + other_ref[...] * (1.0 - first)).astype(BF))
    put(out_ref, 1, NEAR, on(y % 2 == 1, a1))
    put(out_ref, 2, NEAR, on(y >= 2, a2 + a1 * two + a3 * (1.0 - two)))


def far_kernel(pos_ref, a1_ref, a2_ref, a3_ref, out_ref):
    x = pos_ref[0]
    a1, a2, a3 = a1_ref[...].astype(F32), a2_ref[...].astype(F32), a3_ref[...].astype(F32)
    two = jnp.where(x == 2, 1.0, 0.0)
    put(out_ref, 0, FAR, on(x % 2 == 1, a1))
    put(out_ref, 1, FAR, on(x >= 2, a2 + a1 * two + a3 * (1.0 - two)))


def step_kernel(order, first, pos_ref, *refs):
    refs = refs[0 if first else 1 :]
    qw_hbm, acc_hbm, p_hbm, gain_ref = refs[:4]
    count = len(order) * PER
    states = refs[4 : 4 + 2 * len(order)]
    out_hbm, qw_ref, acc_ref, p_ref, o_ref, sems, out_sems = refs[4 + 2 * len(order) :]
    z, core = pos_ref[3], pos_ref[2]
    heads, loads = [], []
    for i in range(count):
        owner = lax.rem(z + order[i // PER] * (2 * core - 1) + SIDE, SIDE)
        h = owner * PER + i % PER
        copies = [
            pltpu.make_async_copy(qw_hbm.at[h], qw_ref.at[i], sems.at[i, 0]),
            pltpu.make_async_copy(p_hbm.at[h], p_ref.at[i], sems.at[i, 1]),
            pltpu.make_async_copy(acc_hbm.at[:, dynamic_cols(h)], acc_ref.at[i], sems.at[i, 2]),
        ]
        for copy in copies:
            copy.start()
        heads.append(h)
        loads.append(copies)
    stores = []
    for i, h in enumerate(heads):
        for copy in loads[i]:
            copy.wait()
        total = acc_ref[i] + jnp.dot(qw_ref[i, :, :DH], p_ref[i], preferred_element_type=F32)
        at = DH
        for part in states[2 * (i // PER) : 2 * (i // PER) + 2]:
            size = part.shape[0] // PER
            rows = slice(i % PER * size, (i % PER + 1) * size)
            total = total + jnp.dot(qw_ref[i, :, at : at + size], part[rows, :], preferred_element_type=F32)
            at += size
        inv = lax.rsqrt(jnp.mean(total * total, axis=-1, keepdims=True) + EPSILON)
        o_ref[i] = (total * inv * gain_ref[pl.ds(h, 1), :]).astype(BF)
        copy = pltpu.make_async_copy(o_ref.at[i], out_hbm.at[:, dynamic_cols(h)], out_sems.at[i])
        copy.start()
        stores.append(copy)
    for copy in stores:
        copy.wait()


def shift(n, s):
    return [(i, (i + s) % n) for i in range(n)]


SWAP = shift(2, 1)
RING = [(z, (z + 1) % 8) for z in range(8)] + [(8 + z, 8 + (z + 7) % 8) for z in range(8)]


def to_others(value, axis):
    a2 = lax.ppermute(value, axis, shift(4, 2))
    a1 = lax.ppermute(value, axis, shift(4, 1))
    a3 = lax.ppermute(value, axis, shift(4, 3))
    return a1, a2, a3


def swap(value):
    return lax.ppermute(value, "core", SWAP)


def body(queries, key_vectors, value_vectors, level_codes, level_table, out_gain):
    tokens = queries.shape[0]
    whole = (tokens, HEADS * DH)
    z = lax.axis_index("z")
    core = lax.axis_index("core").astype(jnp.int32)
    pos = jnp.stack([lax.axis_index("x"), lax.axis_index("y"), core, z]).astype(jnp.int32)
    codes = lax.dynamic_slice_in_dim(level_codes.T, z * tokens, tokens, 1)
    state = (PER * DH, DH)

    queries, key_vectors, value_vectors = (in_hbm(a) for a in (queries, key_vectors, value_vectors))
    states = call(
        state_kernel, sds((HEADS, DH, DH), BF), [HBM_SPEC] * 2, (2 * tokens * HEADS * DH * DH, 3 << 20),
        scratch=[pltpu.VMEM(whole, BF), pltpu.VMEM(whole, BF), DMA((2, LOADS))],
    )(key_vectors, value_vectors)
    gathered = lax.all_to_all(states, "z", split_axis=0, concat_axis=0, tiled=True)

    eye = jnp.eye(LEVELS, dtype=BF) * jnp.where(jnp.arange(LEVELS) == 1, core, 1).astype(BF)[:, None]
    table = jnp.kron(eye, level_table)
    table = jnp.pad(table, ((0, DH - LEVELS * CODES), (0, DH - LEVELS * HEADS)))
    acc, scaled = call(
        local_kernel, (sds(whole, F32), sds((HEADS, tokens, LEVELS * DH), BF)),
        [HBM_SPEC] * 3 + [VMEM_SPEC] * 2, (4 * tokens * tokens * HEADS * DH, 12 << 20),
        out_specs=(HBM_SPEC, HBM_SPEC),
        scratch=[pltpu.VMEM(whole, BF)] * 3 + [
            pltpu.VMEM(whole, F32), pltpu.VMEM((HEADS, tokens, LEVELS * DH), BF),
            DMA((3, LOADS)), DMA((LOADS,)), DMA((LOADS,)),
        ],
    )(queries, key_vectors, value_vectors, codes, table)
    acc, scaled = in_hbm(acc), in_hbm(scaled)
    gathered, acc, scaled = lax.optimization_barrier((gathered, acc, scaled))
    acc, scaled = in_hbm(acc), in_hbm(scaled)

    chunks = gathered.reshape((SIDE,) + state)
    mine = call(total_kernel, sds(state, F32), [VMEM_SPEC], (8 * 2 * DH * DH, 1 << 20))(chunks)
    other = swap(mine)
    prefixes = call(prefix_kernel, sds((SIDE,) + state, BF), [VMEM_SPEC], (8 * 2 * DH * DH, 1 << 20))(chunks)
    prefix = lax.all_to_all(prefixes.reshape(HEADS, DH, DH), "z", split_axis=0, concat_axis=0, tiled=True)
    total, sent = call(pair_kernel, (sds(state, F32), sds(state, BF)), [VMEM_SPEC] * 2, (DH * DH, 1 << 18))(mine, other)
    around = to_others(sent, "y")
    near, _, sent = call(
        near_kernel, (sds((PER * NEAR * DH, DH), BF), sds(state, F32), sds(state, BF)), [SMEM_SPEC] + [VMEM_SPEC] * 6,
        (8 * DH * DH, 1 << 18),
    )(pos, mine, other, total, *around)
    around = to_others(sent, "x")
    far = call(
        far_kernel, sds((PER * FAR * DH, DH), BF), [SMEM_SPEC] + [VMEM_SPEC] * 3, (8 * DH * DH, 1 << 18)
    )(pos, *around)

    def reads(order, arrays, out):
        n = len(order) * PER
        return call(
            functools.partial(step_kernel, order, out is None), sds(whole, BF),
            [SMEM_SPEC] + ([] if out is None else [HBM_SPEC])
            + [HBM_SPEC] * 3 + [VMEM_SPEC] * (1 + len(arrays)),
            (12 * tokens * n * DH * DH, n << 19),
            out_specs=HBM_SPEC,
            scratch=[
                pltpu.VMEM((n, tokens, LEVELS * DH), BF), pltpu.VMEM((n, tokens, DH), F32),
                pltpu.VMEM((n, DH, DH), BF), pltpu.VMEM((n, tokens, DH), BF), DMA((n, 3)), DMA((n,)),
            ],
            alias=None if out is None else {1: 0},
        )(pos, *([] if out is None else [out]), scaled, acc, prefix, out_gain, *arrays)

    a, b = near, far
    held = [((0,), [a, b])]
    for hop in range(1, 5):
        a = lax.ppermute(a, ("core", "z"), RING)
        b = lax.ppermute(b, ("core", "z"), RING)
        held.append(((hop, -hop), [a, b, swap(a), swap(b)]) if hop < 4 else ((hop,), [a, b]))
    out = None
    for hops in ((0, 1), (2,), (3, 4)):
        order = sum((held[hop][0] for hop in hops), ())
        arrays = sum((held[hop][1] for hop in hops), [])
        out = reads(order, arrays, out)
    return out


def solution(mesh):
    grid = Mesh(mesh.devices.reshape(4, 4, 2, 8), ("x", "y", "core", "z"))
    rows = P(("x", "y", "core", "z"), None)
    in_specs = (rows, rows, rows, P(("x", "y", "core"), None), P(), P())


    return jax.shard_map(body, mesh=grid, in_specs=in_specs, out_specs=rows, check_vma=False)
```

```python
import functools

import jax
import jax.numpy as jnp
from jax import lax
from jax.experimental import pallas as pl
from jax.experimental.pallas import tpu as pltpu
from jax.sharding import Mesh, PartitionSpec as P


HEADS = 16
DH = 128
LEVELS = 6
CODES = 16
NEAR = 3
FAR = 2
SIDE = 8
PER = HEADS // SIDE
EPSILON = 1e-06
BF = jnp.bfloat16
F32 = jnp.float32


VMEM_SPEC = pl.BlockSpec(memory_space=pltpu.VMEM)
SMEM_SPEC = pl.BlockSpec(memory_space=pltpu.SMEM)
HBM_SPEC = pl.BlockSpec(memory_space=pltpu.HBM)
DMA = pltpu.SemaphoreType.DMA


def sds(shape, dtype):
    return jax.ShapeDtypeStruct(shape, dtype)


def call(kernel, outs, in_specs, cost, out_specs=None, scratch=(), alias=None):
    return pl.pallas_call(
        kernel,
        out_shape=outs,
        in_specs=in_specs,
        out_specs=jax.tree.map(lambda _: VMEM_SPEC, outs) if out_specs is None else out_specs,
        scratch_shapes=scratch,
        input_output_aliases=alias or {},
        compiler_params=pltpu.CompilerParams(vmem_limit_bytes=20 << 20),
        cost_estimate=pl.CostEstimate(flops=cost[0], bytes_accessed=cost[1], transcendentals=0),
    )


def in_hbm(value):
    return pltpu.with_memory_space_constraint(value, pltpu.HBM)


def head_cols(h):
    return pl.ds(h * DH, DH)


def dynamic_cols(h):
    return pl.ds(pl.multiple_of(h * DH, DH), DH)


LOADS = 4


def state_kernel(k_hbm, v_hbm, s_ref, k_ref, v_ref, sems):
    width = HEADS * DH // LOADS
    copies = []
    for i in range(LOADS):
        cols = pl.ds(i * width, width)
        pair = [
            pltpu.make_async_copy(k_hbm.at[:, cols], k_ref.at[:, cols], sems.at[0, i]),
            pltpu.make_async_copy(v_hbm.at[:, cols], v_ref.at[:, cols], sems.at[1, i]),
        ]
        for copy in pair:
            copy.start()
        copies.append(pair)
    for i in range(LOADS):
        for copy in copies[i]:
            copy.wait()
        for h in range(i * HEADS // LOADS, (i + 1) * HEADS // LOADS):
            s = lax.dot_general(
                k_ref[:, head_cols(h)], v_ref[:, head_cols(h)], (((0,), (0,)), ((), ())),
                preferred_element_type=F32,
            )
            s_ref[h] = s.astype(BF)


def local_kernel(
    q_hbm, k_hbm, v_hbm, codes_ref, table_ref, acc_hbm, qw_hbm, q_ref, k_ref, v_ref, acc_ref, qw_ref, sems, acc_sems, qw_sems
):
    width = HEADS * DH // LOADS
    per = HEADS // LOADS
    copies = []
    for i in range(LOADS):
        cols = pl.ds(i * width, width)
        group = [
            pltpu.make_async_copy(src.at[:, cols], dst.at[:, cols], sems.at[j, i])
            for j, (src, dst) in enumerate(((q_hbm, q_ref), (k_hbm, k_ref), (v_hbm, v_ref)))
        ]
        for copy in group:
            copy.start()
        copies.append(group)
    tokens = q_ref.shape[0]
    code_ids = lax.broadcasted_iota(jnp.int32, (CODES, tokens), 0)
    hits = [codes_ref[l : l + 1, :] == code_ids for l in range(LEVELS)]
    hits = [jnp.where(hit, 1.0, 0.0).astype(BF) for hit in hits]
    hits = jnp.concatenate(hits + [jnp.zeros((DH - LEVELS * CODES, tokens), BF)], axis=0)
    w = lax.dot_general(hits, table_ref[...], (((0,), (0,)), ((), ())), preferred_element_type=F32).astype(BF)
    rows = lax.broadcasted_iota(jnp.int32, (tokens, tokens), 0)
    cols = lax.broadcasted_iota(jnp.int32, (tokens, tokens), 1)
    keep = cols <= rows
    pick = lax.broadcasted_iota(jnp.int32, (DH, LEVELS * DH), 0)
    pick = pick - lax.broadcasted_iota(jnp.int32, (DH, LEVELS * DH), 1) // DH * HEADS
    stores = []
    for i in range(LOADS):
        for copy in copies[i]:
            copy.wait()
        for h in range(i * per, (i + 1) * per):
            spread = jnp.dot(w, jnp.where(pick == h, 1.0, 0.0).astype(BF), preferred_element_type=F32)
            q = q_ref[:, head_cols(h)]
            wide = q.astype(F32)
            for l in range(LEVELS):
                qw_ref[h, :, head_cols(l)] = (spread[:, l * DH : (l + 1) * DH] * wide).astype(BF)
            s = lax.dot_general(q, k_ref[:, head_cols(h)], (((1,), (1,)), ((), ())), preferred_element_type=F32)
            s = jnp.where(keep, s, 0.0).astype(BF)
            part = jnp.dot(s, v_ref[:, head_cols(h)], preferred_element_type=F32)
            acc_ref[:, head_cols(h)] = spread[:, :DH] * part
        cols = pl.ds(i * width, width)
        heads = pl.ds(i * per, per)
        for store in (
            pltpu.make_async_copy(acc_ref.at[:, cols], acc_hbm.at[:, cols], acc_sems.at[i]),
            pltpu.make_async_copy(qw_ref.at[heads], qw_hbm.at[heads], qw_sems.at[i]),
        ):
            store.start()
            stores.append(store)
    for store in stores:
        store.wait()


def total_kernel(r_ref, mine_ref):
    run = r_ref[0].astype(F32)
    for j in range(1, SIDE):
        run = run + r_ref[j].astype(F32)
    mine_ref[...] = run


def prefix_kernel(r_ref, p_ref):
    run = jnp.zeros((PER * DH, DH), F32)
    for j in range(SIDE):
        p_ref[j] = run.astype(BF)
        run = run + r_ref[j].astype(F32)


def pair_kernel(mine_ref, other_ref, total_ref, sent_ref):
    total = mine_ref[...] + other_ref[...]
    total_ref[...] = total
    sent_ref[...] = total.astype(BF)


def on(flag, value):
    return (value * jnp.where(flag, 1.0, 0.0)).astype(BF)


def put(out_refs, l, value):
    for i in range(PER):
        out_refs[i][l * DH : (l + 1) * DH, :] = value[i * DH : (i + 1) * DH, :]


def near_kernel(pos_ref, mine_ref, other_ref, total_ref, a1_ref, a2_ref, a3_ref, *outs):
    y, core = pos_ref[1], pos_ref[2]
    a1, a2, a3 = a1_ref[...].astype(F32), a2_ref[...].astype(F32), a3_ref[...].astype(F32)
    outs[PER][...] = (total_ref[...] + (a1 + a2 + a3)).astype(BF)
    two = jnp.where(y == 2, 1.0, 0.0)
    first = jnp.where(core == 0, 1.0, 0.0)
    put(outs, 0, (mine_ref[...] * first + other_ref[...] * (1.0 - first)).astype(BF))
    put(outs, 1, on(y % 2 == 1, a1))
    put(outs, 2, on(y >= 2, a2 + a1 * two + a3 * (1.0 - two)))


def far_kernel(pos_ref, a1_ref, a2_ref, a3_ref, *outs):
    x = pos_ref[0]
    a1, a2, a3 = a1_ref[...].astype(F32), a2_ref[...].astype(F32), a3_ref[...].astype(F32)
    two = jnp.where(x == 2, 1.0, 0.0)
    put(outs, 0, on(x % 2 == 1, a1))
    put(outs, 1, on(x >= 2, a2 + a1 * two + a3 * (1.0 - two)))


def head_at(pos_ref, order, i):
    owner = lax.rem(pos_ref[3] + order[i // PER] * (2 * pos_ref[2] - 1) + SIDE, SIDE)
    return owner * PER + i % PER


def finish(i, h, total, scaled, at, states, gain_ref, o_ref, out_hbm, out_sems):
    for part in states[2 * i : 2 * i + 2]:
        size = part.shape[0]
        total = total + jnp.dot(scaled[:, at : at + size], part[...], preferred_element_type=F32)
        at += size
    inv = lax.rsqrt(jnp.mean(total * total, axis=-1, keepdims=True) + EPSILON)
    o_ref[i] = (total * inv * gain_ref[pl.ds(h, 1), :]).astype(BF)
    copy = pltpu.make_async_copy(o_ref.at[i], out_hbm.at[:, dynamic_cols(h)], out_sems.at[i])
    copy.start()
    return copy


def step_kernel(order, first, pos_ref, *refs):
    refs = refs[0 if first else 1 :]
    qw_hbm, acc_hbm, p_hbm, gain_ref = refs[:4]
    count = len(order) * PER
    states = refs[4 : 4 + 2 * count]
    out_hbm, qw_ref, acc_ref, p_ref, o_ref, sems, out_sems = refs[4 + 2 * count :]
    loads = []
    for i in range(count):
        h = head_at(pos_ref, order, i)
        copies = [
            pltpu.make_async_copy(qw_hbm.at[h], qw_ref.at[i], sems.at[i, 0]),
            pltpu.make_async_copy(p_hbm.at[h], p_ref.at[i], sems.at[i, 1]),
            pltpu.make_async_copy(acc_hbm.at[:, dynamic_cols(h)], acc_ref.at[i], sems.at[i, 2]),
        ]
        for copy in copies:
            copy.start()
        loads.append(copies)
    stores = []
    for i in range(count):
        for copy in loads[i]:
            copy.wait()
        total = acc_ref[i] + jnp.dot(qw_ref[i, :, :DH], p_ref[i], preferred_element_type=F32)
        stores.append(
            finish(i, head_at(pos_ref, order, i), total, qw_ref.at[i], DH, states, gain_ref, o_ref, out_hbm, out_sems)
        )
    for copy in stores:
        copy.wait()


def load_kernel(order, pos_ref, qw_hbm, acc_hbm, p_hbm, qw_out, acc_out, q_ref, p_ref, sems):
    count = len(order) * PER
    loads = []
    for i in range(count):
        h = head_at(pos_ref, order, i)
        copies = [
            pltpu.make_async_copy(qw_hbm.at[h, :, pl.ds(0, DH)], q_ref.at[i], sems.at[i, 0]),
            pltpu.make_async_copy(p_hbm.at[h], p_ref.at[i], sems.at[i, 1]),
            pltpu.make_async_copy(acc_hbm.at[:, dynamic_cols(h)], acc_out.at[i], sems.at[i, 2]),
            pltpu.make_async_copy(qw_hbm.at[h, :, pl.ds(DH, (LEVELS - 1) * DH)], qw_out.at[i], sems.at[i, 3]),
        ]
        for copy in copies:
            copy.start()
        loads.append(copies)
    for i in range(count):
        for copy in loads[i][:3]:
            copy.wait()
        acc_out[i] = acc_out[i] + jnp.dot(q_ref[i], p_ref[i], preferred_element_type=F32)
    for copies in loads:
        copies[3].wait()


def last_kernel(order, pos_ref, prev_hbm, qw_ref, acc_ref, gain_ref, *refs):
    count = len(order) * PER
    states = refs[: 2 * count]
    out_hbm, o_ref, out_sems = refs[2 * count :]
    stores = [
        finish(
            i, head_at(pos_ref, order, i), acc_ref[i], qw_ref.at[i], 0, states, gain_ref, o_ref, out_hbm, out_sems
        )
        for i in range(count)
    ]
    for copy in stores:
        copy.wait()


def shift(n, s):
    return [(i, (i + s) % n) for i in range(n)]


SWAP = shift(2, 1)
RING = [(z, (z + 1) % 8) for z in range(8)] + [(8 + z, 8 + (z + 7) % 8) for z in range(8)]


def to_others(value, axis):
    a2 = lax.ppermute(value, axis, shift(4, 2))
    a1 = lax.ppermute(value, axis, shift(4, 1))
    a3 = lax.ppermute(value, axis, shift(4, 3))
    return a1, a2, a3


def swap(value):
    return lax.ppermute(value, "core", SWAP)


def body(queries, key_vectors, value_vectors, level_codes, level_table, out_gain):
    tokens = queries.shape[0]
    whole = (tokens, HEADS * DH)
    z = lax.axis_index("z")
    core = lax.axis_index("core").astype(jnp.int32)
    pos = jnp.stack([lax.axis_index("x"), lax.axis_index("y"), core, z]).astype(jnp.int32)
    codes = lax.dynamic_slice_in_dim(level_codes.T, z * tokens, tokens, 1)
    state = (PER * DH, DH)

    queries, key_vectors, value_vectors = (in_hbm(a) for a in (queries, key_vectors, value_vectors))
    states = call(
        state_kernel, sds((HEADS, DH, DH), BF), [HBM_SPEC] * 2, (2 * tokens * HEADS * DH * DH, 3 << 20),
        scratch=[pltpu.VMEM(whole, BF), pltpu.VMEM(whole, BF), DMA((2, LOADS))],
    )(key_vectors, value_vectors)
    gathered = lax.all_to_all(states, "z", split_axis=0, concat_axis=0, tiled=True)

    eye = jnp.eye(LEVELS, dtype=BF) * jnp.where(jnp.arange(LEVELS) == 1, core, 1).astype(BF)[:, None]
    table = jnp.kron(eye, level_table)
    table = jnp.pad(table, ((0, DH - LEVELS * CODES), (0, DH - LEVELS * HEADS)))
    acc, scaled = call(
        local_kernel, (sds(whole, F32), sds((HEADS, tokens, LEVELS * DH), BF)),
        [HBM_SPEC] * 3 + [VMEM_SPEC] * 2, (4 * tokens * tokens * HEADS * DH, 12 << 20),
        out_specs=(HBM_SPEC, HBM_SPEC),
        scratch=[pltpu.VMEM(whole, BF)] * 3 + [
            pltpu.VMEM(whole, F32), pltpu.VMEM((HEADS, tokens, LEVELS * DH), BF),
            DMA((3, LOADS)), DMA((LOADS,)), DMA((LOADS,)),
        ],
    )(queries, key_vectors, value_vectors, codes, table)
    acc, scaled = in_hbm(acc), in_hbm(scaled)
    gathered, acc, scaled = lax.optimization_barrier((gathered, acc, scaled))
    acc, scaled = in_hbm(acc), in_hbm(scaled)

    chunks = gathered.reshape((SIDE,) + state)
    mine = call(total_kernel, sds(state, F32), [VMEM_SPEC], (8 * 2 * DH * DH, 1 << 20))(chunks)
    other = swap(mine)
    prefixes = call(prefix_kernel, sds((SIDE,) + state, BF), [VMEM_SPEC], (8 * 2 * DH * DH, 1 << 20))(chunks)
    prefix = lax.all_to_all(prefixes.reshape(HEADS, DH, DH), "z", split_axis=0, concat_axis=0, tiled=True)
    total, sent = call(pair_kernel, (sds(state, F32), sds(state, BF)), [VMEM_SPEC] * 2, (DH * DH, 1 << 18))(mine, other)
    around = to_others(sent, "y")
    *near, sent = call(
        near_kernel, (sds((NEAR * DH, DH), BF),) * PER + (sds(state, BF),), [SMEM_SPEC] + [VMEM_SPEC] * 6,
        (8 * DH * DH, 1 << 18),
    )(pos, mine, other, total, *around)
    around = to_others(sent, "x")
    far = call(
        far_kernel, (sds((FAR * DH, DH), BF),) * PER, [SMEM_SPEC] + [VMEM_SPEC] * 3, (8 * DH * DH, 1 << 18)
    )(pos, *around)

    near, far = list(near), list(far)

    def paired():
        return [part[i] for i in range(PER) for part in (near, far)]

    held = [((0,), paired())]
    for hop in range(1, 5):
        near = [lax.ppermute(part, ("core", "z"), RING) for part in near]
        far = [lax.ppermute(part, ("core", "z"), RING) for part in far]
        arrays = paired()
        held.append(((hop, -hop), arrays + [swap(a) for a in arrays]) if hop < 4 else ((hop,), arrays))

    out = None
    for hop in range(2):
        order, arrays = held[hop]
        n = len(order) * PER
        out = call(
            functools.partial(step_kernel, order, out is None), sds(whole, BF),
            [SMEM_SPEC] + ([] if out is None else [HBM_SPEC]) + [HBM_SPEC] * 3 + [VMEM_SPEC] * (1 + len(arrays)),
            (12 * tokens * n * DH * DH, n << 19),
            out_specs=HBM_SPEC,
            scratch=[
                pltpu.VMEM((n, tokens, LEVELS * DH), BF), pltpu.VMEM((n, tokens, DH), F32),
                pltpu.VMEM((n, DH, DH), BF), pltpu.VMEM((n, tokens, DH), BF), DMA((n, 3)), DMA((n,)),
            ],
            alias=None if out is None else {1: 0},
        )(pos, *([] if out is None else [out]), scaled, acc, prefix, out_gain, *arrays)
    order = sum((held[hop][0] for hop in (2, 3, 4)), ())
    arrays = sum((held[hop][1] for hop in (2, 3, 4)), [])
    n = len(order) * PER
    scaled, acc = call(
        functools.partial(load_kernel, order),
        (sds((n, tokens, (LEVELS - 1) * DH), BF), sds((n, tokens, DH), F32)),
        [SMEM_SPEC] + [HBM_SPEC] * 3, (2 * tokens * n * DH * DH, n << 19),
        scratch=[pltpu.VMEM((n, tokens, DH), BF), pltpu.VMEM((n, DH, DH), BF), DMA((n, 4))],
    )(pos, scaled, acc, prefix)
    return call(
        functools.partial(last_kernel, order), sds(whole, BF),
        [SMEM_SPEC, HBM_SPEC] + [VMEM_SPEC] * (3 + len(arrays)), (10 * tokens * n * DH * DH, n << 19),
        out_specs=HBM_SPEC, scratch=[pltpu.VMEM((n, tokens, DH), BF), DMA((n,))], alias={1: 0},
    )(pos, out, scaled, acc, out_gain, *arrays)


def solution(mesh):
    grid = Mesh(mesh.devices.reshape(4, 4, 2, 8), ("x", "y", "core", "z"))
    rows = P(("x", "y", "core", "z"), None)
    in_specs = (rows, rows, rows, P(("x", "y", "core"), None), P(), P())

    return jax.shard_map(body, mesh=grid, in_specs=in_specs, out_specs=rows, check_vma=False)
```

```python
import functools

import jax
import jax.numpy as jnp
from jax import lax
from jax.experimental import pallas as pl
from jax.experimental.pallas import tpu as pltpu
from jax.sharding import Mesh, PartitionSpec as P


HEADS = 16
DH = 128
LEVELS = 6
CODES = 16
NEAR = 3
FAR = 2
SIDE = 8
PER = HEADS // SIDE
EPSILON = 1e-06
BF = jnp.bfloat16
F32 = jnp.float32


VMEM_SPEC = pl.BlockSpec(memory_space=pltpu.VMEM)
SMEM_SPEC = pl.BlockSpec(memory_space=pltpu.SMEM)
HBM_SPEC = pl.BlockSpec(memory_space=pltpu.HBM)
DMA = pltpu.SemaphoreType.DMA


def sds(shape, dtype):
    return jax.ShapeDtypeStruct(shape, dtype)


def call(kernel, outs, in_specs, cost, out_specs=None, scratch=(), alias=None):
    return pl.pallas_call(
        kernel,
        out_shape=outs,
        in_specs=in_specs,
        out_specs=jax.tree.map(lambda _: VMEM_SPEC, outs) if out_specs is None else out_specs,
        scratch_shapes=scratch,
        input_output_aliases=alias or {},
        compiler_params=pltpu.CompilerParams(vmem_limit_bytes=20 << 20),
        cost_estimate=pl.CostEstimate(flops=cost[0], bytes_accessed=cost[1], transcendentals=0),
    )


def in_hbm(value):
    return pltpu.with_memory_space_constraint(value, pltpu.HBM)


def head_cols(h):
    return pl.ds(h * DH, DH)


def dynamic_cols(h):
    return pl.ds(pl.multiple_of(h * DH, DH), DH)


LOADS = 4


def state_kernel(k_hbm, v_hbm, s_hbm, k_ref, v_ref, s_ref, sems, out_sems):
    width = HEADS * DH // LOADS
    per = HEADS // LOADS
    copies, stores = [], []
    for i in range(LOADS):
        cols = pl.ds(i * width, width)
        pair = [
            pltpu.make_async_copy(k_hbm.at[:, cols], k_ref.at[:, cols], sems.at[0, i]),
            pltpu.make_async_copy(v_hbm.at[:, cols], v_ref.at[:, cols], sems.at[1, i]),
        ]
        for copy in pair:
            copy.start()
        copies.append(pair)
    for i in range(LOADS):
        for copy in copies[i]:
            copy.wait()
        for h in range(i * per, (i + 1) * per):
            s = lax.dot_general(
                k_ref[:, head_cols(h)], v_ref[:, head_cols(h)], (((0,), (0,)), ((), ())),
                preferred_element_type=F32,
            )
            s_ref[h] = s.astype(BF)
        heads = pl.ds(i * per, per)
        store = pltpu.make_async_copy(s_ref.at[heads], s_hbm.at[heads], out_sems.at[i])
        store.start()
        stores.append(store)
    for store in stores:
        store.wait()


def local_kernel(
    q_hbm, k_hbm, v_hbm, codes_ref, table_ref, acc_hbm, qw_hbm, q_ref, k_ref, v_ref, acc_ref, qw_ref, sems, acc_sems, qw_sems
):
    width = HEADS * DH // LOADS
    per = HEADS // LOADS
    copies = []
    for i in range(LOADS):
        cols = pl.ds(i * width, width)
        group = [
            pltpu.make_async_copy(src.at[:, cols], dst.at[:, cols], sems.at[j, i])
            for j, (src, dst) in enumerate(((q_hbm, q_ref), (k_hbm, k_ref), (v_hbm, v_ref)))
        ]
        for copy in group:
            copy.start()
        copies.append(group)
    tokens = q_ref.shape[0]
    code_ids = lax.broadcasted_iota(jnp.int32, (CODES, tokens), 0)
    hits = [codes_ref[l : l + 1, :] == code_ids for l in range(LEVELS)]
    hits = [jnp.where(hit, 1.0, 0.0).astype(BF) for hit in hits]
    hits = jnp.concatenate(hits + [jnp.zeros((DH - LEVELS * CODES, tokens), BF)], axis=0)
    w = lax.dot_general(hits, table_ref[...], (((0,), (0,)), ((), ())), preferred_element_type=F32).astype(BF)
    rows = lax.broadcasted_iota(jnp.int32, (tokens, tokens), 0)
    cols = lax.broadcasted_iota(jnp.int32, (tokens, tokens), 1)
    keep = cols <= rows
    pick = lax.broadcasted_iota(jnp.int32, (DH, LEVELS * DH), 0)
    pick = pick - lax.broadcasted_iota(jnp.int32, (DH, LEVELS * DH), 1) // DH * HEADS
    stores = []
    for i in range(LOADS):
        for copy in copies[i]:
            copy.wait()
        for h in range(i * per, (i + 1) * per):
            spread = jnp.dot(w, jnp.where(pick == h, 1.0, 0.0).astype(BF), preferred_element_type=F32)
            q = q_ref[:, head_cols(h)]
            wide = q.astype(F32)
            for l in range(LEVELS):
                qw_ref[h, :, head_cols(l)] = (spread[:, l * DH : (l + 1) * DH] * wide).astype(BF)
            s = lax.dot_general(q, k_ref[:, head_cols(h)], (((1,), (1,)), ((), ())), preferred_element_type=F32)
            s = jnp.where(keep, s, 0.0).astype(BF)
            part = jnp.dot(s, v_ref[:, head_cols(h)], preferred_element_type=F32)
            acc_ref[:, head_cols(h)] = spread[:, :DH] * part
        cols = pl.ds(i * width, width)
        heads = pl.ds(i * per, per)
        for store in (
            pltpu.make_async_copy(acc_ref.at[:, cols], acc_hbm.at[:, cols], acc_sems.at[i]),
            pltpu.make_async_copy(qw_ref.at[heads], qw_hbm.at[heads], qw_sems.at[i]),
        ):
            store.start()
            stores.append(store)
    for store in stores:
        store.wait()


def total_kernel(r_ref, mine_ref):
    run = r_ref[0].astype(F32)
    for j in range(1, SIDE):
        run = run + r_ref[j].astype(F32)
    mine_ref[...] = run


def prefix_kernel(r_ref, p_ref):
    run = jnp.zeros((PER * DH, DH), F32)
    for j in range(SIDE):
        p_ref[j] = run.astype(BF)
        run = run + r_ref[j].astype(F32)


def pair_kernel(mine_ref, other_ref, total_ref, sent_ref):
    total = mine_ref[...] + other_ref[...]
    total_ref[...] = total
    sent_ref[...] = total.astype(BF)


def on(flag, value):
    return (value * jnp.where(flag, 1.0, 0.0)).astype(BF)


def put(out_ref, l, value):
    size = out_ref.shape[0] // PER
    for i in range(PER):
        at = i * size + l * DH
        out_ref[at : at + DH, :] = value[i * DH : (i + 1) * DH, :]


def near_kernel(pos_ref, mine_ref, other_ref, total_ref, a1_ref, a2_ref, a3_ref, out_ref, sent_ref):
    y, core = pos_ref[1], pos_ref[2]
    a1, a2, a3 = a1_ref[...].astype(F32), a2_ref[...].astype(F32), a3_ref[...].astype(F32)
    sent_ref[...] = (total_ref[...] + (a1 + a2 + a3)).astype(BF)
    two = jnp.where(y == 2, 1.0, 0.0)
    first = jnp.where(core == 0, 1.0, 0.0)
    put(out_ref, 0, (mine_ref[...] * first + other_ref[...] * (1.0 - first)).astype(BF))
    put(out_ref, 1, on(y % 2 == 1, a1))
    put(out_ref, 2, on(y >= 2, a2 + a1 * two + a3 * (1.0 - two)))


def far_kernel(pos_ref, a1_ref, a2_ref, a3_ref, out_ref):
    x = pos_ref[0]
    a1, a2, a3 = a1_ref[...].astype(F32), a2_ref[...].astype(F32), a3_ref[...].astype(F32)
    two = jnp.where(x == 2, 1.0, 0.0)
    put(out_ref, 0, on(x % 2 == 1, a1))
    put(out_ref, 1, on(x >= 2, a2 + a1 * two + a3 * (1.0 - two)))


def head_at(pos_ref, order, i):
    owner = lax.rem(pos_ref[3] + order[i // PER] * (2 * pos_ref[2] - 1) + SIDE, SIDE)
    return owner * PER + i % PER


def finish(i, h, total, scaled, at, states, gain_ref, o_ref, out_hbm, out_sems):
    for part in states[i // PER * 2 : i // PER * 2 + 2]:
        size = part.shape[0] // PER
        rows = slice(i % PER * size, (i % PER + 1) * size)
        total = total + jnp.dot(scaled[:, at : at + size], part[rows, :], preferred_element_type=F32)
        at += size
    inv = lax.rsqrt(jnp.mean(total * total, axis=-1, keepdims=True) + EPSILON)
    o_ref[i] = (total * inv * gain_ref[pl.ds(h, 1), :]).astype(BF)
    copy = pltpu.make_async_copy(o_ref.at[i], out_hbm.at[:, dynamic_cols(h)], out_sems.at[i])
    copy.start()
    return copy


def step_kernel(order, first, pos_ref, *refs):
    refs = refs[0 if first else 1 :]
    qw_hbm, acc_hbm, p_hbm, gain_ref = refs[:4]
    count = len(order) * PER
    states = refs[4 : 4 + 2 * len(order)]
    out_hbm, qw_ref, acc_ref, p_ref, o_ref, sems, out_sems = refs[4 + 2 * len(order) :]
    loads = []
    for i in range(count):
        h = head_at(pos_ref, order, i)
        copies = [
            pltpu.make_async_copy(qw_hbm.at[h], qw_ref.at[i], sems.at[i, 0]),
            pltpu.make_async_copy(p_hbm.at[h], p_ref.at[i], sems.at[i, 1]),
            pltpu.make_async_copy(acc_hbm.at[:, dynamic_cols(h)], acc_ref.at[i], sems.at[i, 2]),
        ]
        for copy in copies:
            copy.start()
        loads.append(copies)
    stores = []
    for i in range(count):
        for copy in loads[i]:
            copy.wait()
        total = acc_ref[i] + jnp.dot(qw_ref[i, :, :DH], p_ref[i], preferred_element_type=F32)
        stores.append(
            finish(i, head_at(pos_ref, order, i), total, qw_ref.at[i], DH, states, gain_ref, o_ref, out_hbm, out_sems)
        )
    for copy in stores:
        copy.wait()


def load_kernel(order, pos_ref, qw_hbm, acc_hbm, p_hbm, qw_out, acc_out, q_ref, p_ref, sems):
    count = len(order) * PER
    loads = []
    for i in range(count):
        h = head_at(pos_ref, order, i)
        copies = [
            pltpu.make_async_copy(qw_hbm.at[h, :, pl.ds(0, DH)], q_ref.at[i], sems.at[i, 0]),
            pltpu.make_async_copy(p_hbm.at[h], p_ref.at[i], sems.at[i, 1]),
            pltpu.make_async_copy(acc_hbm.at[:, dynamic_cols(h)], acc_out.at[i], sems.at[i, 2]),
            pltpu.make_async_copy(qw_hbm.at[h, :, pl.ds(DH, (LEVELS - 1) * DH)], qw_out.at[i], sems.at[i, 3]),
        ]
        for copy in copies:
            copy.start()
        loads.append(copies)
    for i in range(count):
        for copy in loads[i][:3]:
            copy.wait()
        acc_out[i] = acc_out[i] + jnp.dot(q_ref[i], p_ref[i], preferred_element_type=F32)
    for copies in loads:
        copies[3].wait()


def last_kernel(order, pos_ref, prev_hbm, qw_ref, acc_ref, gain_ref, *refs):
    count = len(order) * PER
    states = refs[: 2 * len(order)]
    out_hbm, o_ref, out_sems = refs[2 * len(order) :]
    stores = [
        finish(
            i, head_at(pos_ref, order, i), acc_ref[i], qw_ref.at[i], 0, states, gain_ref, o_ref, out_hbm, out_sems
        )
        for i in range(count)
    ]
    for copy in stores:
        copy.wait()


def shift(n, s):
    return [(i, (i + s) % n) for i in range(n)]


SWAP = shift(2, 1)
RING = [(z, (z + 1) % 8) for z in range(8)] + [(8 + z, 8 + (z + 7) % 8) for z in range(8)]


def to_others(value, axis):
    a2 = lax.ppermute(value, axis, shift(4, 2))
    a1 = lax.ppermute(value, axis, shift(4, 1))
    a3 = lax.ppermute(value, axis, shift(4, 3))
    return a1, a2, a3


def swap(value):
    return lax.ppermute(value, "core", SWAP)


def body(queries, key_vectors, value_vectors, level_codes, level_table, out_gain):
    tokens = queries.shape[0]
    whole = (tokens, HEADS * DH)
    z = lax.axis_index("z")
    core = lax.axis_index("core").astype(jnp.int32)
    pos = jnp.stack([lax.axis_index("x"), lax.axis_index("y"), core, z]).astype(jnp.int32)
    codes = lax.dynamic_slice_in_dim(level_codes.T, z * tokens, tokens, 1)
    state = (PER * DH, DH)

    queries, key_vectors, value_vectors = (in_hbm(a) for a in (queries, key_vectors, value_vectors))
    states = call(
        state_kernel, sds((HEADS, DH, DH), BF), [HBM_SPEC] * 2, (2 * tokens * HEADS * DH * DH, 3 << 20),
        out_specs=HBM_SPEC,
        scratch=[
            pltpu.VMEM(whole, BF), pltpu.VMEM(whole, BF), pltpu.VMEM((HEADS, DH, DH), BF), DMA((2, LOADS)), DMA((LOADS,)),
        ],
    )(key_vectors, value_vectors)
    gathered = lax.all_to_all(states, "z", split_axis=0, concat_axis=0, tiled=True)

    eye = jnp.eye(LEVELS, dtype=BF) * jnp.where(jnp.arange(LEVELS) == 1, core, 1).astype(BF)[:, None]
    table = jnp.kron(eye, level_table)
    table = jnp.pad(table, ((0, DH - LEVELS * CODES), (0, DH - LEVELS * HEADS)))
    acc, scaled = call(
        local_kernel, (sds(whole, F32), sds((HEADS, tokens, LEVELS * DH), BF)),
        [HBM_SPEC] * 3 + [VMEM_SPEC] * 2, (4 * tokens * tokens * HEADS * DH, 12 << 20),
        out_specs=(HBM_SPEC, HBM_SPEC),
        scratch=[pltpu.VMEM(whole, BF)] * 3 + [
            pltpu.VMEM(whole, F32), pltpu.VMEM((HEADS, tokens, LEVELS * DH), BF),
            DMA((3, LOADS)), DMA((LOADS,)), DMA((LOADS,)),
        ],
    )(queries, key_vectors, value_vectors, codes, table)
    acc, scaled = in_hbm(acc), in_hbm(scaled)
    gathered, acc, scaled = lax.optimization_barrier((gathered, acc, scaled))
    acc, scaled = in_hbm(acc), in_hbm(scaled)

    chunks = gathered.reshape((SIDE,) + state)
    mine = call(total_kernel, sds(state, F32), [VMEM_SPEC], (8 * 2 * DH * DH, 1 << 20))(chunks)
    other = swap(mine)
    prefixes = call(prefix_kernel, sds((SIDE,) + state, BF), [VMEM_SPEC], (8 * 2 * DH * DH, 1 << 20))(chunks)
    prefix = lax.all_to_all(prefixes.reshape(HEADS, DH, DH), "z", split_axis=0, concat_axis=0, tiled=True)
    total, sent = call(pair_kernel, (sds(state, F32), sds(state, BF)), [VMEM_SPEC] * 2, (DH * DH, 1 << 18))(mine, other)
    around = to_others(sent, "y")
    near, sent = call(
        near_kernel, (sds((PER * NEAR * DH, DH), BF), sds(state, BF)), [SMEM_SPEC] + [VMEM_SPEC] * 6,
        (8 * DH * DH, 1 << 18),
    )(pos, mine, other, total, *around)
    around = to_others(sent, "x")
    far = call(
        far_kernel, sds((PER * FAR * DH, DH), BF), [SMEM_SPEC] + [VMEM_SPEC] * 3, (8 * DH * DH, 1 << 18)
    )(pos, *around)

    held = [((0,), [near, far])]
    for hop in range(1, 5):
        near = lax.ppermute(near, ("core", "z"), RING)
        far = lax.ppermute(far, ("core", "z"), RING)
        held.append(((hop, -hop), [near, far, swap(near), swap(far)]) if hop < 4 else ((hop,), [near, far]))

    out = None
    for hop in range(2):
        order, arrays = held[hop]
        n = len(order) * PER
        out = call(
            functools.partial(step_kernel, order, out is None), sds(whole, BF),
            [SMEM_SPEC] + ([] if out is None else [HBM_SPEC]) + [HBM_SPEC] * 3 + [VMEM_SPEC] * (1 + len(arrays)),
            (12 * tokens * n * DH * DH, n << 19),
            out_specs=HBM_SPEC,
            scratch=[
                pltpu.VMEM((n, tokens, LEVELS * DH), BF), pltpu.VMEM((n, tokens, DH), F32),
                pltpu.VMEM((n, DH, DH), BF), pltpu.VMEM((n, tokens, DH), BF), DMA((n, 3)), DMA((n,)),
            ],
            alias=None if out is None else {1: 0},
        )(pos, *([] if out is None else [out]), scaled, acc, prefix, out_gain, *arrays)
    order = sum((held[hop][0] for hop in (2, 3, 4)), ())
    arrays = sum((held[hop][1] for hop in (2, 3, 4)), [])
    n = len(order) * PER
    scaled, acc = call(
        functools.partial(load_kernel, order),
        (sds((n, tokens, (LEVELS - 1) * DH), BF), sds((n, tokens, DH), F32)),
        [SMEM_SPEC] + [HBM_SPEC] * 3, (2 * tokens * n * DH * DH, n << 19),
        scratch=[pltpu.VMEM((n, tokens, DH), BF), pltpu.VMEM((n, DH, DH), BF), DMA((n, 4))],
    )(pos, scaled, acc, prefix)
    return call(
        functools.partial(last_kernel, order), sds(whole, BF),
        [SMEM_SPEC, HBM_SPEC] + [VMEM_SPEC] * (3 + len(arrays)), (10 * tokens * n * DH * DH, n << 19),
        out_specs=HBM_SPEC, scratch=[pltpu.VMEM((n, tokens, DH), BF), DMA((n,))], alias={1: 0},
    )(pos, out, scaled, acc, out_gain, *arrays)


def solution(mesh):
    grid = Mesh(mesh.devices.reshape(4, 4, 2, 8), ("x", "y", "core", "z"))
    rows = P(("x", "y", "core", "z"), None)
    in_specs = (rows, rows, rows, P(("x", "y", "core"), None), P(), P())

    return jax.shard_map(body, mesh=grid, in_specs=in_specs, out_specs=rows, check_vma=False)
```

```python
import functools

import jax
import jax.numpy as jnp
from jax import lax
from jax.experimental import pallas as pl
from jax.experimental.pallas import tpu as pltpu
from jax.sharding import Mesh, PartitionSpec as P


HEADS = 16
DH = 128
LEVELS = 6
CODES = 16
NEAR = 3
FAR = 2
SIDE = 8
PER = HEADS // SIDE
EPSILON = 1e-06
BF = jnp.bfloat16
F32 = jnp.float32


VMEM_SPEC = pl.BlockSpec(memory_space=pltpu.VMEM)
SMEM_SPEC = pl.BlockSpec(memory_space=pltpu.SMEM)
HBM_SPEC = pl.BlockSpec(memory_space=pltpu.HBM)
DMA = pltpu.SemaphoreType.DMA


def sds(shape, dtype):
    return jax.ShapeDtypeStruct(shape, dtype)


def call(kernel, outs, in_specs, cost, out_specs=None, scratch=(), alias=None):
    return pl.pallas_call(
        kernel,
        out_shape=outs,
        in_specs=in_specs,
        out_specs=jax.tree.map(lambda _: VMEM_SPEC, outs) if out_specs is None else out_specs,
        scratch_shapes=scratch,
        input_output_aliases=alias or {},
        compiler_params=pltpu.CompilerParams(vmem_limit_bytes=20 << 20),
        cost_estimate=pl.CostEstimate(flops=cost[0], bytes_accessed=cost[1], transcendentals=0),
    )


def in_hbm(value):
    return pltpu.with_memory_space_constraint(value, pltpu.HBM)


def head_cols(h):
    return pl.ds(h * DH, DH)


def dynamic_cols(h):
    return pl.ds(pl.multiple_of(h * DH, DH), DH)


LOADS = 2


def state_kernel(k_hbm, v_hbm, s_hbm, k_ref, v_ref, s_ref, sems, out_sems):
    width = HEADS * DH // LOADS
    per = HEADS // LOADS
    copies, stores = [], []
    for i in range(LOADS):
        cols = pl.ds(i * width, width)
        pair = [
            pltpu.make_async_copy(k_hbm.at[:, cols], k_ref.at[:, cols], sems.at[0, i]),
            pltpu.make_async_copy(v_hbm.at[:, cols], v_ref.at[:, cols], sems.at[1, i]),
        ]
        for copy in pair:
            copy.start()
        copies.append(pair)
    for i in range(LOADS):
        for copy in copies[i]:
            copy.wait()
        for h in range(i * per, (i + 1) * per):
            s = lax.dot_general(
                k_ref[:, head_cols(h)], v_ref[:, head_cols(h)], (((0,), (0,)), ((), ())),
                preferred_element_type=F32,
            )
            s_ref[h] = s.astype(BF)
        heads = pl.ds(i * per, per)
        store = pltpu.make_async_copy(s_ref.at[heads], s_hbm.at[heads], out_sems.at[i])
        store.start()
        stores.append(store)
    for store in stores:
        store.wait()


def local_kernel(
    q_hbm, k_hbm, v_hbm, codes_ref, table_ref, acc_hbm, qw_hbm, q_ref, k_ref, v_ref, acc_ref, qw_ref, sems, acc_sems, qw_sems
):
    width = HEADS * DH // LOADS
    per = HEADS // LOADS
    copies = []
    for i in range(LOADS):
        cols = pl.ds(i * width, width)
        group = [
            pltpu.make_async_copy(src.at[:, cols], dst.at[:, cols], sems.at[j, i])
            for j, (src, dst) in enumerate(((q_hbm, q_ref), (k_hbm, k_ref), (v_hbm, v_ref)))
        ]
        for copy in group:
            copy.start()
        copies.append(group)
    tokens = q_ref.shape[0]
    code_ids = lax.broadcasted_iota(jnp.int32, (CODES, tokens), 0)
    hits = [codes_ref[l : l + 1, :] == code_ids for l in range(LEVELS)]
    hits = [jnp.where(hit, 1.0, 0.0).astype(BF) for hit in hits]
    hits = jnp.concatenate(hits + [jnp.zeros((DH - LEVELS * CODES, tokens), BF)], axis=0)
    w = lax.dot_general(hits, table_ref[...], (((0,), (0,)), ((), ())), preferred_element_type=F32).astype(BF)
    rows = lax.broadcasted_iota(jnp.int32, (tokens, tokens), 0)
    cols = lax.broadcasted_iota(jnp.int32, (tokens, tokens), 1)
    keep = cols <= rows
    pick = lax.broadcasted_iota(jnp.int32, (DH, LEVELS * DH), 0)
    pick = pick - lax.broadcasted_iota(jnp.int32, (DH, LEVELS * DH), 1) // DH * HEADS
    stores = []
    for i in range(LOADS):
        for copy in copies[i]:
            copy.wait()
        for h in range(i * per, (i + 1) * per):
            spread = jnp.dot(w, jnp.where(pick == h, 1.0, 0.0).astype(BF), preferred_element_type=F32)
            q = q_ref[:, head_cols(h)]
            wide = q.astype(F32)
            for l in range(LEVELS):
                qw_ref[h, :, head_cols(l)] = (spread[:, l * DH : (l + 1) * DH] * wide).astype(BF)
            s = lax.dot_general(q, k_ref[:, head_cols(h)], (((1,), (1,)), ((), ())), preferred_element_type=F32)
            s = jnp.where(keep, s, 0.0).astype(BF)
            part = jnp.dot(s, v_ref[:, head_cols(h)], preferred_element_type=F32)
            acc_ref[:, head_cols(h)] = spread[:, :DH] * part
        cols = pl.ds(i * width, width)
        heads = pl.ds(i * per, per)
        for store in (
            pltpu.make_async_copy(acc_ref.at[:, cols], acc_hbm.at[:, cols], acc_sems.at[i]),
            pltpu.make_async_copy(qw_ref.at[heads], qw_hbm.at[heads], qw_sems.at[i]),
        ):
            store.start()
            stores.append(store)
    for store in stores:
        store.wait()


def total_kernel(r_ref, mine_ref):
    run = r_ref[0].astype(F32)
    for j in range(1, SIDE):
        run = run + r_ref[j].astype(F32)
    mine_ref[...] = run


def prefix_kernel(r_ref, p_ref):
    run = jnp.zeros((PER * DH, DH), F32)
    for j in range(SIDE):
        p_ref[j] = run.astype(BF)
        run = run + r_ref[j].astype(F32)


def pair_kernel(mine_ref, other_ref, total_ref, sent_ref):
    total = mine_ref[...] + other_ref[...]
    total_ref[...] = total
    sent_ref[...] = total.astype(BF)


def on(flag, value):
    return (value * jnp.where(flag, 1.0, 0.0)).astype(BF)


def put(out_ref, l, value):
    size = out_ref.shape[0] // PER
    for i in range(PER):
        at = i * size + l * DH
        out_ref[at : at + DH, :] = value[i * DH : (i + 1) * DH, :]


def near_kernel(pos_ref, mine_ref, other_ref, total_ref, a1_ref, a2_ref, a3_ref, out_ref, sent_ref):
    y, core = pos_ref[1], pos_ref[2]
    a1, a2, a3 = a1_ref[...].astype(F32), a2_ref[...].astype(F32), a3_ref[...].astype(F32)
    sent_ref[...] = (total_ref[...] + (a1 + a2 + a3)).astype(BF)
    two = jnp.where(y == 2, 1.0, 0.0)
    first = jnp.where(core == 0, 1.0, 0.0)
    put(out_ref, 0, (mine_ref[...] * first + other_ref[...] * (1.0 - first)).astype(BF))
    put(out_ref, 1, on(y % 2 == 1, a1))
    put(out_ref, 2, on(y >= 2, a2 + a1 * two + a3 * (1.0 - two)))


def far_kernel(pos_ref, a1_ref, a2_ref, a3_ref, out_ref):
    x = pos_ref[0]
    a1, a2, a3 = a1_ref[...].astype(F32), a2_ref[...].astype(F32), a3_ref[...].astype(F32)
    two = jnp.where(x == 2, 1.0, 0.0)
    put(out_ref, 0, on(x % 2 == 1, a1))
    put(out_ref, 1, on(x >= 2, a2 + a1 * two + a3 * (1.0 - two)))


def head_at(pos_ref, order, i):
    owner = lax.rem(pos_ref[3] + order[i // PER] * (2 * pos_ref[2] - 1) + SIDE, SIDE)
    return owner * PER + i % PER


def finish(i, h, total, scaled, at, states, gain_ref, o_ref, out_hbm, out_sems):
    for part in states[i // PER * 2 : i // PER * 2 + 2]:
        size = part.shape[0] // PER
        rows = slice(i % PER * size, (i % PER + 1) * size)
        total = total + jnp.dot(scaled[:, at : at + size], part[rows, :], preferred_element_type=F32)
        at += size
    inv = lax.rsqrt(jnp.mean(total * total, axis=-1, keepdims=True) + EPSILON)
    o_ref[i] = (total * inv * gain_ref[pl.ds(h, 1), :]).astype(BF)
    copy = pltpu.make_async_copy(o_ref.at[i], out_hbm.at[:, dynamic_cols(h)], out_sems.at[i])
    copy.start()
    return copy


def load_kernel(order, pos_ref, qw_hbm, acc_hbm, p_hbm, qw_out, acc_out, q_ref, p_ref, sems):
    count = len(order) * PER
    loads = []
    for i in range(count):
        h = head_at(pos_ref, order, i)
        copies = [
            pltpu.make_async_copy(qw_hbm.at[h, :, pl.ds(0, DH)], q_ref.at[i], sems.at[i, 0]),
            pltpu.make_async_copy(p_hbm.at[h], p_ref.at[i], sems.at[i, 1]),
            pltpu.make_async_copy(acc_hbm.at[:, dynamic_cols(h)], acc_out.at[i], sems.at[i, 2]),
            pltpu.make_async_copy(qw_hbm.at[h, :, pl.ds(DH, (LEVELS - 1) * DH)], qw_out.at[i], sems.at[i, 3]),
        ]
        for copy in copies:
            copy.start()
        loads.append(copies)
    for i in range(count):
        for copy in loads[i][:3]:
            copy.wait()
        acc_out[i] = acc_out[i] + jnp.dot(q_ref[i], p_ref[i], preferred_element_type=F32)
    for copies in loads:
        copies[3].wait()


def read_kernel(order, skip, pos_ref, *refs):
    refs = refs[1 if skip else 0 :]
    qw_ref, acc_ref, gain_ref = refs[:3]
    states = refs[3 : 3 + 2 * len(order)]
    out_hbm, o_ref, out_sems = refs[3 + 2 * len(order) :]
    stores = []
    for i in range(len(order) * PER):
        h = head_at(pos_ref, order, i)
        stores.append(
            finish(i, h, acc_ref[skip + i], qw_ref.at[skip + i], 0, states, gain_ref, o_ref, out_hbm, out_sems)
        )
    for copy in stores:
        copy.wait()


def shift(n, s):
    return [(i, (i + s) % n) for i in range(n)]


SWAP = shift(2, 1)
RING = [(z, (z + 1) % 8) for z in range(8)] + [(8 + z, 8 + (z + 7) % 8) for z in range(8)]


def to_others(value, axis):
    a2 = lax.ppermute(value, axis, shift(4, 2))
    a1 = lax.ppermute(value, axis, shift(4, 1))
    a3 = lax.ppermute(value, axis, shift(4, 3))
    return a1, a2, a3


def swap(value):
    return lax.ppermute(value, "core", SWAP)


def body(queries, key_vectors, value_vectors, level_codes, level_table, out_gain):
    tokens = queries.shape[0]
    whole = (tokens, HEADS * DH)
    z = lax.axis_index("z")
    core = lax.axis_index("core").astype(jnp.int32)
    pos = jnp.stack([lax.axis_index("x"), lax.axis_index("y"), core, z]).astype(jnp.int32)
    codes = lax.dynamic_slice_in_dim(level_codes.T, z * tokens, tokens, 1)
    state = (PER * DH, DH)

    queries, key_vectors, value_vectors = (in_hbm(a) for a in (queries, key_vectors, value_vectors))
    states = call(
        state_kernel, sds((HEADS, DH, DH), BF), [HBM_SPEC] * 2, (2 * tokens * HEADS * DH * DH, 3 << 20),
        out_specs=HBM_SPEC,
        scratch=[
            pltpu.VMEM(whole, BF), pltpu.VMEM(whole, BF), pltpu.VMEM((HEADS, DH, DH), BF), DMA((2, LOADS)), DMA((LOADS,)),
        ],
    )(key_vectors, value_vectors)
    gathered = lax.all_to_all(states, "z", split_axis=0, concat_axis=0, tiled=True)

    eye = jnp.eye(LEVELS, dtype=BF) * jnp.where(jnp.arange(LEVELS) == 1, core, 1).astype(BF)[:, None]
    table = jnp.kron(eye, level_table)
    table = jnp.pad(table, ((0, DH - LEVELS * CODES), (0, DH - LEVELS * HEADS)))
    acc, scaled = call(
        local_kernel, (sds(whole, F32), sds((HEADS, tokens, LEVELS * DH), BF)),
        [HBM_SPEC] * 3 + [VMEM_SPEC] * 2, (4 * tokens * tokens * HEADS * DH, 12 << 20),
        out_specs=(HBM_SPEC, HBM_SPEC),
        scratch=[pltpu.VMEM(whole, BF)] * 3 + [
            pltpu.VMEM(whole, F32), pltpu.VMEM((HEADS, tokens, LEVELS * DH), BF),
            DMA((3, LOADS)), DMA((LOADS,)), DMA((LOADS,)),
        ],
    )(queries, key_vectors, value_vectors, codes, table)
    acc, scaled = in_hbm(acc), in_hbm(scaled)
    gathered, acc, scaled = lax.optimization_barrier((gathered, acc, scaled))
    acc, scaled = in_hbm(acc), in_hbm(scaled)

    chunks = gathered.reshape((SIDE,) + state)
    mine = call(total_kernel, sds(state, F32), [VMEM_SPEC], (8 * 2 * DH * DH, 1 << 20))(chunks)
    other = swap(mine)
    prefixes = call(prefix_kernel, sds((SIDE,) + state, BF), [VMEM_SPEC], (8 * 2 * DH * DH, 1 << 20))(chunks)
    prefix = lax.all_to_all(prefixes.reshape(HEADS, DH, DH), "z", split_axis=0, concat_axis=0, tiled=True)
    total, sent = call(pair_kernel, (sds(state, F32), sds(state, BF)), [VMEM_SPEC] * 2, (DH * DH, 1 << 18))(mine, other)
    around = to_others(sent, "y")
    near, sent = call(
        near_kernel, (sds((PER * NEAR * DH, DH), BF), sds(state, BF)), [SMEM_SPEC] + [VMEM_SPEC] * 6,
        (8 * DH * DH, 1 << 18),
    )(pos, mine, other, total, *around)
    around = to_others(sent, "x")
    far = call(
        far_kernel, sds((PER * FAR * DH, DH), BF), [SMEM_SPEC] + [VMEM_SPEC] * 3, (8 * DH * DH, 1 << 18)
    )(pos, *around)

    held = [((0,), [near, far])]
    for hop in range(1, 5):
        near = lax.ppermute(near, ("core", "z"), RING)
        far = lax.ppermute(far, ("core", "z"), RING)
        held.append(((hop, -hop), [near, far, swap(near), swap(far)]) if hop < 4 else ((hop,), [near, far]))

    def order_of(hops):
        return sum((held[hop][0] for hop in hops), ())

    scaled, acc = call(
        functools.partial(load_kernel, order_of(range(5))),
        (sds((HEADS, tokens, (LEVELS - 1) * DH), BF), sds((HEADS, tokens, DH), F32)),
        [SMEM_SPEC] + [HBM_SPEC] * 3, (2 * tokens * HEADS * DH * DH, 9 << 20),
        scratch=[pltpu.VMEM((HEADS, tokens, DH), BF), pltpu.VMEM((HEADS, DH, DH), BF), DMA((HEADS, 4))],
    )(pos, scaled, acc, prefix)
    out, skip = None, 0
    for hops in ((0, 1, 2), (3, 4)):
        order = order_of(hops)
        arrays = sum((held[hop][1] for hop in hops), [])
        n = len(order) * PER
        out = call(
            functools.partial(read_kernel, order, skip), sds(whole, BF),
            [SMEM_SPEC] + ([HBM_SPEC] if skip else []) + [VMEM_SPEC] * (3 + len(arrays)),
            (10 * tokens * n * DH * DH, n << 19),
            out_specs=HBM_SPEC, scratch=[pltpu.VMEM((n, tokens, DH), BF), DMA((n,))],
            alias={1: 0} if skip else None,
        )(pos, *([out] if skip else []), scaled, acc, out_gain, *arrays)
        skip += n
    return out


def solution(mesh):
    grid = Mesh(mesh.devices.reshape(4, 4, 2, 8), ("x", "y", "core", "z"))
    rows = P(("x", "y", "core", "z"), None)
    in_specs = (rows, rows, rows, P(("x", "y", "core"), None), P(), P())

    return jax.shard_map(body, mesh=grid, in_specs=in_specs, out_specs=rows, check_vma=False)
```
